32 devices in a mesh: groups: 2 (over x), sensor: 16 (over z, y, core).
Axes of the slice: x: 2, y: 2, z: 4, core: 2. Of those that a mesh axis runs over, the one named last changes fastest.
Arguments:
- series: float32 [288, 1536], P(None, ('groups', 'sensor')), parts along dimension 1, may hold values from -6 to 6
- starts: int32 [2], P('groups'), parts along dimension 0, may hold values from 0 to 276
- sensor_order: int32 [1536], P(('groups', 'sensor')), parts along dimension 0, may hold values from 0 to 767, each once
- emb_src: float32 [10, 1536], P(None, ('groups', 'sensor')), parts along dimension 1, may hold values from -4.4 to 330
- emb_dst: float32 [10, 1536], P(None, ('groups', 'sensor')), parts along dimension 1, may hold values from -4.4 to 4.4
- start_proj: float32 [2, 32], replicated, may hold values from -4 to 4
- conv_weight: bfloat16 [64, 64], replicated, may hold values from -0.75 to 0.75
- mix_weight: bfloat16 [96, 32], replicated, may hold values from -0.625 to 0.625
- out_grad: bfloat16 [1536, 384], P(('groups', 'sensor')), parts along dimension 0, may hold values from -0.59765625 to 0.59765625
Outputs:
- layer_out: bfloat16 [1536, 384], P(('groups', 'sensor')), parts along dimension 0
- grad_src: float32 [10, 1536], P(None, ('groups', 'sensor')), parts along dimension 1
- grad_dst: float32 [10, 1536], P(None, ('groups', 'sensor')), parts along dimension 1
- grad_mix: float32 [192, 32], P('groups'), parts along dimension 0
The draws below stay inside these ranges and needn't reach their ends.
There are 2 independent parts, one for each index of `groups`. The reference program is written for one: setup_inputs(seed, part) draws one part's arguments, and reference() takes and returns one part's arrays. A program takes and returns all parts, laid end to end along the dimension named above; an argument that names none is the same for every part. Nothing has to cross between parts.
All inputs are finite; a program needn't handle non-finite values.
Results may differ from the reference program's by a relative error of at most 0.035.
Values may be sent and summed in bfloat16 or wider, within the bound.
A program may use at most 64 MiB of HBM per device.

```python
import math
import jax
import jax.numpy as jnp
from jax import lax

C = 32
EMB = 10
STEPS = 12
WIN = 1
TIME = 288
SENSORS = 768
FEAT = 384


def embedding_pair(key):
    keys = jax.random.split(jax.random.fold_in(key, 11), 5)
    dims = jnp.arange(EMB)[:, None]
    source = jax.random.truncated_normal(keys[0], -4.0, 4.0, (EMB, SENSORS), jnp.float32) * 0.816
    target = jax.random.truncated_normal(keys[1], -4.0, 4.0, (EMB, SENSORS), jnp.float32) * 0.816
    bulk_cols = jax.random.uniform(keys[2], (SENSORS,), jnp.float32) < 0.5
    bulk_level = jax.random.uniform(keys[3], (SENSORS,), jnp.float32, 1.5, 1.75)
    row_level = jax.random.uniform(keys[4], (SENSORS,), jnp.float32, 0.85, 1.15)
    target = jnp.where(bulk_cols[None, :], target * 0.1, target)
    source = jnp.where(dims == 1, row_level[None, :], source)
    target = jnp.where(dims == 1, jnp.where(bulk_cols[None, :], bulk_level[None, :], 0.0), target)
    return (source, target)


def draw_emb_src(key, part):
    return embedding_pair(key)[0]


def draw_emb_dst(key, part):
    return embedding_pair(key)[1]


def steps_of(own_key, shape, cuts, low, top_value):
    level = 1.0
    for dim, parts in cuts:
        heights = jax.random.uniform(jax.random.fold_in(jax.random.fold_in(own_key, 6), dim), (parts,), jnp.float32, low / len(cuts), top_value / len(cuts))
        level = level * jnp.repeat(jnp.exp(heights), shape[dim] // parts).reshape((-1,) + (1,) * (len(shape) - 1 - dim))
    return level


def gaussian(own_key, extent, spread, bound, cuts=(), kind=jnp.bfloat16):
    drawn = jax.random.normal(own_key, extent, jnp.float32) * spread
    if len(cuts) > 0:
        drawn = steps_of(own_key, extent, cuts, -0.22, 0.18) * drawn
    return jnp.clip(drawn, min=-bound, max=bound).astype(kind)


def setup_inputs(seed: int = 0, part: int = 0) -> dict:
    seeds = jax.random.split(jax.random.key(seed), 10)
    own_keys = jax.random.split(jax.random.fold_in(seeds[9], part), 10)
    return {
        "series": gaussian(own_keys[0], (TIME, SENSORS), 1.0, 6.0, ((1, 16),), jnp.float32),
        "starts": jax.random.randint(own_keys[1], (WIN,), 0, TIME - STEPS + 1).astype(jnp.int32),
        "sensor_order": jax.random.permutation(own_keys[2], SENSORS).astype(jnp.int32),
        "emb_src": draw_emb_src(jax.random.fold_in(jax.random.fold_in(seeds[9], part), 71), part),
        "emb_dst": draw_emb_dst(jax.random.fold_in(jax.random.fold_in(seeds[9], part), 71), part),
        "start_proj": gaussian(seeds[5], (2, C), 1.0, 4.0, (), jnp.float32),
        "conv_weight": gaussian(seeds[6], (2 * C, 2 * C), (2 * C) ** -0.5, 0.75),
        "mix_weight": gaussian(seeds[7], (3 * C, C), (3 * C) ** -0.5, 0.625),
        "out_grad": gaussian(own_keys[8], (SENSORS, FEAT), 0.1, 0.59765625, ((0, 16),)),
    }


highest = lax.Precision.HIGHEST

def front(readings, start_proj, conv_weight):
    sensors_here = readings.shape[0]
    channels = start_proj.shape[1]
    padded = jnp.concatenate([jnp.zeros(readings.shape[:-1] + (1,), jnp.float32), readings], axis=-1)
    inputs = (padded[..., None] * start_proj[0] + start_proj[1]).astype(jnp.bfloat16)
    paired = jnp.concatenate([inputs[:, :, :-1, :], inputs[:, :, 1:, :]], axis=-1).reshape(-1, 2 * channels)
    gate_terms = jnp.dot(paired, conv_weight, preferred_element_type=jnp.float32)
    hidden = (jnp.tanh(gate_terms[:, :channels]) * jax.nn.sigmoid(gate_terms[:, channels:])).astype(jnp.bfloat16)
    return (hidden.reshape(sensors_here, -1), inputs[:, :, 1:, :].reshape(sensors_here, -1))

def mixing(residual, hidden, diffused, second, mix_weight):
    channels = mix_weight.shape[1]
    stacked = jnp.concatenate([member.reshape(-1, channels) for member in (hidden, diffused, second)], axis=1)
    summed = residual.reshape(-1, channels).astype(jnp.float32) + jnp.dot(stacked, mix_weight, preferred_element_type=jnp.float32)
    return (summed.astype(jnp.bfloat16).reshape(hidden.shape[0], -1), stacked)

def channel_grads(out_grad, mix_weight):
    channels = mix_weight.shape[1]
    row_count = out_grad.shape[0]
    flat_grad = out_grad.reshape(-1, channels)
    dims = (((1,), (1,)), ((), ()))
    grad_once = lax.dot_general(flat_grad, mix_weight[channels:2 * channels], dims, preferred_element_type=jnp.float32)
    grad_twice = lax.dot_general(flat_grad, mix_weight[2 * channels:], dims, preferred_element_type=jnp.float32)
    return (grad_once.astype(jnp.bfloat16).reshape(row_count, -1), grad_twice.astype(jnp.bfloat16).reshape(row_count, -1))

def tile_probs(rows_emb, cols_emb, row_max, row_total):
    scores = jnp.einsum('ei,ej->ij', rows_emb, cols_emb, precision=highest)
    shares = jnp.exp(jnp.maximum(scores, 0.0) - row_max[:, None]) / row_total[:, None]
    return (scores, shares)

def pair_dot(left, right):
    return lax.dot_general(left, right, (((1,), (1,)), ((), ())), preferred_element_type=jnp.float32)

def reference(series, starts, sensor_order, emb_src, emb_dst, start_proj, conv_weight, mix_weight, out_grad):
    windows = jax.vmap(lambda first_step: lax.dynamic_slice_in_dim(series, first_step, STEPS, 0))(starts)
    readings = jnp.transpose(jnp.take(windows, sensor_order, axis=2), (2, 0, 1))
    hidden, residual = front(readings, start_proj, conv_weight)
    span_size = math.gcd(SENSORS, 512)
    blocks = jnp.arange(SENSORS // span_size, dtype=jnp.int32)

    def rows_of(values_in, position, axis_dim):
        return lax.dynamic_slice_in_dim(values_in, position * span_size, span_size, axis_dim)

    def stats_block(position):
        scores = jnp.maximum(jnp.einsum('ei,ej->ij', rows_of(emb_src, position, 1), emb_dst, precision=highest), 0.0)
        best_score = lax.optimization_barrier(jnp.max(scores, axis=1))
        return (best_score, lax.optimization_barrier(jnp.sum(jnp.exp(scores - best_score[:, None]), axis=1)))
    best_rows, total_rows = lax.map(stats_block, blocks)
    row_max = best_rows.reshape(-1)
    row_total = total_rows.reshape(-1)

    def apply_rows(features):

        def one_block(position):
            scores, shares = tile_probs(rows_of(emb_src, position, 1), emb_dst, rows_of(row_max, position, 0), rows_of(row_total, position, 0))
            return jnp.dot(shares.astype(jnp.bfloat16), features, preferred_element_type=jnp.float32)
        return lax.map(one_block, blocks).reshape(SENSORS, -1)
    diffused_full = apply_rows(hidden)
    diffused = diffused_full.astype(jnp.bfloat16)
    second_full = apply_rows(diffused)
    second = second_full.astype(jnp.bfloat16)
    layer_out, stacked = mixing(residual, hidden, diffused, second, mix_weight)
    grad_mix = lax.dot_general(stacked, out_grad.reshape(-1, C), (((0,), (0,)), ((), ())), preferred_element_type=jnp.float32)
    grad_once, grad_twice = channel_grads(out_grad, mix_weight)

    def back_block(position):
        scores, shares = tile_probs(emb_src, rows_of(emb_dst, position, 1), row_max, row_total)
        return lax.dot_general(shares.astype(jnp.bfloat16), grad_twice, (((0,), (0,)), ((), ())), preferred_element_type=jnp.float32)
    adjoint_sum = lax.map(back_block, blocks).reshape(SENSORS, -1)
    carried = (grad_once.astype(jnp.float32) + adjoint_sum).astype(jnp.bfloat16)
    row_delta = lax.optimization_barrier(jnp.sum(grad_twice.astype(jnp.float32) * second_full + carried.astype(jnp.float32) * diffused_full, axis=1))

    def score_grad(src_part, row_top, row_sum, twice_part, carried_part, delta_part, dst_part, diff_part, hidden_part):
        scores, shares = tile_probs(src_part, dst_part, row_top, row_sum)
        dweights = pair_dot(twice_part, diff_part) + pair_dot(carried_part, hidden_part) - delta_part[:, None]
        return jnp.where(scores > 0.0, shares * dweights, 0.0)

    def src_block(position):
        dscore = score_grad(rows_of(emb_src, position, 1), rows_of(row_max, position, 0), rows_of(row_total, position, 0), rows_of(grad_twice, position, 0), rows_of(carried, position, 0), rows_of(row_delta, position, 0), emb_dst, diffused, hidden)
        return jnp.einsum('ej,ij->ei', emb_dst, dscore, precision=highest)

    def dst_block(position):
        dscore = score_grad(emb_src, row_max, row_total, grad_twice, carried, row_delta, rows_of(emb_dst, position, 1), rows_of(diffused, position, 0), rows_of(hidden, position, 0))
        return jnp.einsum('ei,ij->ej', emb_src, dscore, precision=highest)
    grad_src = jnp.transpose(lax.map(src_block, blocks), (1, 0, 2)).reshape(EMB, -1)
    grad_dst = jnp.transpose(lax.map(dst_block, blocks), (1, 0, 2)).reshape(EMB, -1)
    return (layer_out, grad_src, grad_dst, grad_mix)
```

```python
import math

import jax
import jax.numpy as jnp
from jax import lax
from jax.experimental import pallas as pl
from jax.experimental.pallas import tpu as pltpu
from jax.sharding import PartitionSpec as P

STEPS = 12


highest = lax.Precision.HIGHEST


def front(readings, start_proj, conv_weight):
    sensors_here = readings.shape[0]
    channels = start_proj.shape[1]
    padded = jnp.concatenate(
        [jnp.zeros(readings.shape[:-1] + (1,), jnp.float32), readings], axis=-1
    )
    inputs = (padded[..., None] * start_proj[0] + start_proj[1]).astype(jnp.bfloat16)
    paired = jnp.concatenate([inputs[:, :, :-1, :], inputs[:, :, 1:, :]], axis=-1).reshape(
        -1, 2 * channels
    )
    gate_terms = jnp.dot(paired, conv_weight, preferred_element_type=jnp.float32)
    hidden = (jnp.tanh(gate_terms[:, :channels]) * jax.nn.sigmoid(gate_terms[:, channels:])).astype(
        jnp.bfloat16
    )
    return (hidden.reshape(sensors_here, -1), inputs[:, :, 1:, :].reshape(sensors_here, -1))


def mixing(residual, hidden, diffused, second, mix_weight):
    channels = mix_weight.shape[1]
    stacked = jnp.concatenate(
        [member.reshape(-1, channels) for member in (hidden, diffused, second)], axis=1
    )
    summed = residual.reshape(-1, channels).astype(jnp.float32) + jnp.dot(
        stacked, mix_weight, preferred_element_type=jnp.float32
    )
    return (summed.astype(jnp.bfloat16).reshape(hidden.shape[0], -1), stacked)


def channel_grads(out_grad, mix_weight):
    channels = mix_weight.shape[1]
    row_count = out_grad.shape[0]
    flat_grad = out_grad.reshape(-1, channels)
    dims = (((1,), (1,)), ((), ()))
    grad_once = lax.dot_general(
        flat_grad, mix_weight[channels : 2 * channels], dims, preferred_element_type=jnp.float32
    )
    grad_twice = lax.dot_general(
        flat_grad, mix_weight[2 * channels :], dims, preferred_element_type=jnp.float32
    )
    return (
        grad_once.astype(jnp.bfloat16).reshape(row_count, -1),
        grad_twice.astype(jnp.bfloat16).reshape(row_count, -1),
    )


def tile_probs(rows_emb, cols_emb, row_max, row_total):
    scores = jnp.einsum("ei,ej->ij", rows_emb, cols_emb, precision=highest)
    shares = jnp.exp(jnp.maximum(scores, 0.0) - row_max[:, None]) / row_total[:, None]
    return (scores, shares)


def pair_dot(left, right):
    return lax.dot_general(
        left, right, (((1,), (1,)), ((), ())), preferred_element_type=jnp.float32
    )


def in_blocks(step_fn, status, members, axis_dim):
    amount = members[0].shape[axis_dim]
    span_size = math.gcd(amount, 512)

    def advance(position, current):
        opening = position * span_size
        sliced = tuple(
            (lax.dynamic_slice_in_dim(member, opening, span_size, axis_dim) for member in members)
        )
        return step_fn(current, sliced, opening)

    return lax.fori_loop(0, amount // span_size, advance, status)


def score_grads(status, emb_src, cols_dst, offset, scores, shares, dweights):
    grad_rows, grad_cols = status
    dscore = jnp.where(scores > 0.0, shares * dweights, 0.0)
    grad_rows = grad_rows + jnp.einsum("ej,ij->ei", cols_dst, dscore, precision=highest)
    span_size = dscore.shape[1]
    current = lax.dynamic_slice_in_dim(grad_cols, offset, span_size, 1)
    added = current + jnp.einsum("ei,ij->ej", emb_src, dscore, precision=highest)
    return (grad_rows, lax.dynamic_update_slice_in_dim(grad_cols, added, offset, 1))


def per_device(
    series, starts, sensor_order, emb_src, emb_dst, start_proj, conv_weight, mix_weight, out_grad
):
    local_rows = sensor_order.shape[0]
    embed_dim = emb_src.shape[0]
    channels = start_proj.shape[1]
    all_rows = local_rows * lax.axis_size("sensor")
    windows = jax.vmap(lambda first_step: lax.dynamic_slice_in_dim(series, first_step, STEPS, 0))(
        starts
    )
    flat_windows = windows.reshape(-1, local_rows)
    window_rows = flat_windows.shape[0]

    def pick_step(status, members, offset):
        readings_sum, dst_all = status
        block_windows, block_dst = members
        span_size = block_windows.shape[1]
        onehot = (sensor_order[:, None] == offset + lax.iota(jnp.int32, span_size)[None, :]).astype(
            jnp.float32
        )
        readings_sum = readings_sum + jnp.einsum(
            "wj,pj->wp", block_windows, onehot, precision=highest
        )
        return (readings_sum, lax.dynamic_update_slice_in_dim(dst_all, block_dst, offset, 1))

    readings_sum, dst_all = in_blocks(
        pick_step,
        (
            jnp.zeros((window_rows, local_rows), jnp.float32),
            jnp.zeros((embed_dim, all_rows), jnp.float32),
        ),
        (
            lax.all_gather(flat_windows, "sensor", axis=1, tiled=True),
            lax.all_gather(emb_dst, "sensor", axis=1, tiled=True),
        ),
        1,
    )
    readings = readings_sum.T.reshape(local_rows, -1, STEPS)
    hidden, residual = front(readings, start_proj, conv_weight)
    feat_cols = hidden.shape[1]
    span_all = math.gcd(all_rows, 512)

    def stat_step(position, current):
        best_score, summed = current
        cols_dst = lax.dynamic_slice_in_dim(dst_all, position * span_all, span_all, 1)
        scores = jnp.maximum(jnp.einsum("ei,ej->ij", emb_src, cols_dst, precision=highest), 0.0)
        new_best = jnp.maximum(best_score, jnp.max(scores, axis=1))
        summed = summed * jnp.exp(best_score - new_best) + jnp.sum(
            jnp.exp(scores - new_best[:, None]), axis=1
        )
        return (new_best, summed)

    row_max, row_total = lax.fori_loop(
        0,
        all_rows // span_all,
        stat_step,
        (jnp.zeros((local_rows,), jnp.float32), jnp.zeros((local_rows,), jnp.float32)),
    )
    grad_once, grad_twice = channel_grads(out_grad, mix_weight)

    def spread_step(status, members, offset):
        block_feat = members[0]
        cols_dst = lax.dynamic_slice_in_dim(dst_all, offset, block_feat.shape[0], 1)
        scores, shares = tile_probs(emb_src, cols_dst, row_max, row_total)
        return status + jnp.dot(
            shares.astype(jnp.bfloat16), block_feat, preferred_element_type=jnp.float32
        )

    first_init = jnp.zeros((local_rows, feat_cols), jnp.float32)
    first_result = in_blocks(
        spread_step, first_init, (lax.all_gather(hidden, "sensor", axis=0, tiled=True),), 0
    )
    diffused = first_result.astype(jnp.bfloat16)

    def plain_step(status, members, offset):
        accumulated, grad_rows, grad_cols = status
        return (spread_step(accumulated, members, offset), grad_rows, grad_cols)

    second_init = (
        jnp.zeros((local_rows, feat_cols), jnp.float32),
        jnp.zeros((embed_dim, local_rows), jnp.float32),
        jnp.zeros((embed_dim, all_rows), jnp.float32),
    )
    second_result = in_blocks(
        plain_step, second_init, (lax.all_gather(diffused, "sensor", axis=0, tiled=True),), 0
    )
    second_full, grad_rows, grad_cols = second_result
    second = second_full.astype(jnp.bfloat16)
    layer_out, stacked = mixing(residual, hidden, diffused, second, mix_weight)
    mix_part = lax.dot_general(
        stacked,
        out_grad.reshape(-1, channels),
        (((0,), (0,)), ((), ())),
        preferred_element_type=jnp.float32,
    )
    span_size = math.gcd(lax.axis_size("sensor") * local_rows, 512)

    def piece_term(position):
        cols_dst = lax.dynamic_slice_in_dim(dst_all, position * span_size, span_size, 1)
        scores, shares = tile_probs(emb_src, cols_dst, row_max, row_total)
        return lax.dot_general(
            shares.astype(jnp.bfloat16),
            grad_twice,
            (((0,), (0,)), ((), ())),
            preferred_element_type=jnp.float32,
        )

    adjoint_sum = lax.psum_scatter(
        lax.map(
            piece_term,
            jnp.arange(lax.axis_size("sensor") * local_rows // span_size, dtype=jnp.int32),
        ).reshape(lax.axis_size("sensor") * local_rows, -1),
        "sensor",
        scatter_dimension=0,
        tiled=True,
    )
    carried = (grad_once.astype(jnp.float32) + adjoint_sum).astype(jnp.bfloat16)
    row_delta = jnp.sum(
        grad_twice.astype(jnp.float32) * second_full + carried.astype(jnp.float32) * first_result,
        axis=1,
    )

    def pair_step(status, members, offset):
        block_hidden, block_diff = members
        cols_dst = lax.dynamic_slice_in_dim(dst_all, offset, block_hidden.shape[0], 1)
        scores, shares = tile_probs(emb_src, cols_dst, row_max, row_total)
        dweights = (
            pair_dot(grad_twice, block_diff) + pair_dot(carried, block_hidden) - row_delta[:, None]
        )
        return score_grads(status, emb_src, cols_dst, offset, scores, shares, dweights)

    grad_rows, grad_cols = in_blocks(
        pair_step,
        (grad_rows, grad_cols),
        (
            lax.all_gather(hidden, "sensor", axis=0, tiled=True),
            lax.all_gather(diffused, "sensor", axis=0, tiled=True),
        ),
        0,
    )
    grad_dst = lax.psum_scatter(grad_cols, "sensor", scatter_dimension=1, tiled=True)
    grad_mix = lax.psum(mix_part, "sensor")
    return (layer_out, grad_rows, grad_dst, grad_mix)


PIECE = 16
QUARTERS = 3
NT = (((1,), (1,)), ((), ()))
TN = (((0,), (0,)), ((), ()))
f32 = jnp.float32
bf16 = jnp.bfloat16


def iota(shape, dim):
    return lax.broadcasted_iota(jnp.int32, shape, dim)


def ones_where(mask):
    return jnp.where(mask, 1.0, 0.0).astype(bf16)


def nn(left, right):
    return jnp.dot(left, right, preferred_element_type=f32)


def nt(left, right):
    return lax.dot_general(left, right, NT, preferred_element_type=f32)


def tn(left, right):
    return lax.dot_general(left, right, TN, preferred_element_type=f32)


def halves(value):
    high = value.astype(bf16)
    return high, (value - high.astype(f32)).astype(bf16)


def thirds(value):
    high, middle = halves(value)
    return high, middle, (value - high.astype(f32) - middle.astype(f32)).astype(bf16)


def selection(q):
    col = iota((1, 384), 1)
    tile, lane = col >> 7, col & 127
    u, e = lane >> 4, lane & 15
    left = jnp.where((u == 2) | (u == 5), 1, jnp.where(u == 4, 2, 0)) * 128 + e
    right = jnp.where((u == 1) | (u == 5), 1, jnp.where(u == 3, 2, 0)) * 128 + e + 10
    window = u * 128 + e + 20
    wanted = jnp.where(tile == 0, left, jnp.where(tile == 1, right, window))
    blocks, width = jnp.where(tile == 2, 3, 6), jnp.where(tile == 2, 12, 10)
    wanted = jnp.where((u < blocks) & (e < width), wanted + 40 * q, -1)
    number = jnp.where(col == 320, 32 + 40 * q, -1)
    row = iota((384, 384), 0)
    return ones_where((row == wanted) | ((row & 127) == number))


def layer_kernel(
    n, starts, series, order, src, dst, start_proj, conv, mix, out_grad,
    layer_out, grad_src, grad_dst, grad_mix,
    packed, small, grads, left_emb, right_emb, window_f, window_b, hidden, residual,
    adj, diff_full, diffused, second_full, second, once, twice, carried, stats,
    small_send, small_recv, big_send, big_recv, pass_send, pass_recv,
):
    me = lax.axis_index("sensor")
    rows_q = PIECE * n
    total = QUARTERS * rows_q
    barrier = pltpu.get_barrier_semaphore()
    for k in range(1, n):
        pl.semaphore_signal(
            barrier, inc=1, device_id={"sensor": lax.rem(me + k, n)},
            device_id_type=pl.DeviceIdType.MESH,
        )
    mine = pl.multiple_of(me * PIECE, PIECE)

    window = series[pl.ds(starts[0], STEPS), :]
    block = jnp.concatenate(
        [src[...], dst[...], window, order[...].astype(f32), jnp.zeros((7, 48), f32)], axis=0
    )
    packed[...] = jnp.zeros_like(packed)
    for q in range(QUARTERS):
        packed[40 * q : 40 * q + 40, 0:PIECE] = block[:, PIECE * q : PIECE * (q + 1)]
    small[pl.ds(mine, PIECE), :] = packed[...].T[0:PIECE, :]
    for q in range(QUARTERS):
        grads[q, pl.ds(mine, PIECE), :] = out_grad[PIECE * q : PIECE * (q + 1), :]

    pl.semaphore_wait(barrier, n - 1)

    def remote(where, send, recv, peer):
        return pltpu.make_async_remote_copy(
            src_ref=where, dst_ref=where, send_sem=send, recv_sem=recv,
            device_id={"sensor": peer}, device_id_type=pl.DeviceIdType.MESH,
        )

    small_copies = []
    for k in range(1, n):
        copy = remote(
            small.at[pl.ds(mine, PIECE), :], small_send.at[k], small_recv.at[k],
            lax.rem(me + k, n),
        )
        copy.start()
        small_copies.append(copy)
    sibling = me + 1 - 2 * lax.rem(me, 2)
    big_copies = []
    for k in range(n // 2):
        copy = remote(
            grads.at[:, pl.ds(mine, PIECE), :], big_send.at[k], big_recv.at[k],
            sibling if k == 0 else lax.rem(me + 2 * k, n),
        )
        copy.start()
        big_copies.append(copy)

    spread = ones_where(iota((256, 64), 1) == (iota((256, 64), 0) >> 7) * 32 + (iota((256, 64), 0) & 31))
    gather = ones_where(iota((64, 256), 0) == (iota((64, 256), 1) >> 7) * 32 + (iota((64, 256), 1) & 31))
    conv_big = nn(nn(spread, conv[...]).astype(bf16), gather)
    conv_big = jnp.where(
        ((iota((256, 256), 0) & 127) >> 5) == ((iota((256, 256), 1) & 127) >> 5), conv_big, 0.0
    ).astype(bf16)
    spread = ones_where(iota((384, 96), 1) == (iota((384, 96), 0) >> 7) * 32 + (iota((384, 96), 0) & 31))
    gather = ones_where(iota((32, 128), 0) == (iota((32, 128), 1) & 31))
    mix_big = nn(nn(spread, mix[...]).astype(bf16), gather)
    mix_big = jnp.where(
        ((iota((384, 128), 0) & 127) >> 5) == (iota((384, 128), 1) >> 5), mix_big, 0.0
    ).astype(bf16)
    proj = jnp.concatenate([start_proj[...]] * 4, axis=1)
    weight, bias = proj[0:1, :], proj[1:2, :]
    at = iota((128, 768), 0)
    col = iota((128, 768), 1)
    step = jnp.where(col < 384, (col >> 5) - 1, (col - 384) >> 5)
    expand = ones_where(((at & 15) == step) & (at < 48))
    numbers = jnp.concatenate(
        [
            48 * (iota((1, rows_q), 1) >> 4) + PIECE * q + (iota((1, rows_q), 1) & 15)
            for q in range(QUARTERS)
        ],
        axis=1,
    ).astype(f32)

    for copy in small_copies:
        copy.wait_recv()

    parts = jnp.concatenate(thirds(small[...]), axis=1)
    for q in range(QUARTERS):
        taken = nn(parts, selection(q))
        rows = slice(q * rows_q, (q + 1) * rows_q)
        left_emb[rows, :] = taken[:, 0:128].astype(bf16)
        right_emb[rows, :] = taken[:, 128:256].astype(bf16)
        window_f[rows, :] = taken[:, 256:384]
        window_b[rows, :] = taken[:, 256:384].astype(bf16)

    def chunk(q):
        return pl.ds(pl.multiple_of(q * rows_q, rows_q), rows_q)

    def front_step(q, carry):
        rows = chunk(q)
        onehot = ones_where(window_f[rows, 64:65] == numbers)
        picked = nn(onehot, window_b[...]).astype(bf16)
        wide = nn(picked, expand)
        for b in range(3):
            lanes = slice(128 * b, 128 * (b + 1))
            before = (wide[:, 128 * b : 128 * (b + 1)] * weight + bias).astype(bf16)
            after = (wide[:, 384 + 128 * b : 512 + 128 * b] * weight + bias).astype(bf16)
            residual[rows, lanes] = after
            terms = nn(jnp.concatenate([before, after], axis=1), conv_big)
            gated = jnp.tanh(terms[:, :128]) * (0.5 * jnp.tanh(0.5 * terms[:, 128:]) + 0.5)
            hidden[rows, lanes] = gated.astype(bf16)
        return carry

    lax.fori_loop(0, QUARTERS, front_step, 0)

    def first_step(q, carry):
        rows = chunk(q)
        positive = jnp.maximum(nt(left_emb[rows, :], right_emb[...]), 0.0)
        top = jnp.max(positive, axis=1, keepdims=True)
        terms = jnp.exp(positive - top)
        inverse = 1.0 / jnp.sum(terms, axis=1, keepdims=True)
        weights = (terms * inverse).astype(bf16)
        adj[rows, :] = weights
        stats[rows, 0:1] = top
        stats[rows, 1:2] = inverse
        result = nn(weights, hidden[...])
        diff_full[rows, :] = result
        diffused[rows, :] = result.astype(bf16)
        return carry

    lax.fori_loop(0, QUARTERS, first_step, 0)

    pass_copies = []
    for k in range(1, n // 2):
        big_copies[k].wait_recv()
        origin = pl.multiple_of(lax.rem(me + n - 2 * k, n) * PIECE, PIECE)
        copy = remote(
            grads.at[:, pl.ds(origin, PIECE), :], pass_send.at[k], pass_recv.at[k], sibling
        )
        copy.start()
        pass_copies.append(copy)

    def second_step(q, carry):
        rows = chunk(q)
        result = nn(adj[rows, :], diffused[...])
        second_full[rows, :] = result
        second[rows, :] = result.astype(bf16)
        return carry

    lax.fori_loop(0, QUARTERS, second_step, 0)

    big_copies[0].wait_recv()
    for copy in pass_copies:
        copy.wait_recv()

    def channel_step(q, carry):
        rows = chunk(q)
        given = grads[q]
        for b in range(3):
            lanes = slice(128 * b, 128 * (b + 1))
            both = nt(given[:, lanes], mix_big[128:384, :]).astype(bf16)
            once[rows, lanes] = both[:, :128]
            twice[rows, lanes] = both[:, 128:]
        return carry

    lax.fori_loop(0, QUARTERS, channel_step, 0)

    def adjoint_step(q, carry):
        rows = chunk(q)
        back = tn(adj[:, rows], twice[...])
        total_grad = (once[rows, :].astype(f32) + back).astype(bf16)
        carried[rows, :] = total_grad
        delta = twice[rows, :].astype(f32) * second_full[rows, :] + total_grad.astype(
            f32
        ) * diff_full[rows, :]
        stats[rows, 2:3] = jnp.sum(delta, axis=1, keepdims=True)
        return carry

    lax.fori_loop(0, QUARTERS, adjoint_step, 0)

    def own(ref):
        return jnp.concatenate(
            [
                ref[pl.ds(pl.multiple_of(q * rows_q + me * PIECE, PIECE), PIECE), :]
                for q in range(QUARTERS)
            ],
            axis=0,
        )

    own_hidden, own_diff, own_second = own(hidden), own(diffused), own(second)
    own_left, own_right, own_stats = own(left_emb), own(right_emb), own(stats)
    own_residual = own(residual)
    for b in range(3):
        lanes = slice(128 * b, 128 * (b + 1))
        features = jnp.concatenate(
            [own_hidden[:, lanes], own_diff[:, lanes], own_second[:, lanes]], axis=1
        )
        layer_out[:, lanes] = (own_residual[:, lanes].astype(f32) + nn(features, mix_big)).astype(
            bf16
        )

    def score_grad(scores, stat, products):
        shares = jnp.exp(jnp.maximum(scores, 0.0) - stat[:, 0:1]) * stat[:, 1:2]
        return halves(jnp.where(scores > 0.0, shares * (products - stat[:, 2:3]), 0.0))

    high, low = score_grad(
        nt(own_left, right_emb[...]),
        own_stats,
        nt(own(twice), diffused[...]) + nt(own(carried), hidden[...]),
    )
    summed = (nn(high, right_emb[...]) + nn(low, right_emb[...])).T
    grad_src[...] = summed[0:10, :] + summed[16:26, :] + summed[48:58, :]

    high, low = score_grad(
        nt(left_emb[...], own_right),
        stats[...],
        nt(twice[...], own_diff) + nt(carried[...], own_hidden),
    )
    summed = tn(left_emb[...], high) + tn(left_emb[...], low)
    grad_dst[...] = summed[0:10, :] + summed[32:42, :] + summed[64:74, :]

    mixed = jnp.zeros((128, 384), f32)
    for b in range(3):
        lanes = slice(128 * b, 128 * (b + 1))
        features = jnp.concatenate([hidden[:, lanes], diffused[:, lanes], second[:, lanes]], axis=1)
        mixed = mixed + tn(grads[:, :, lanes].reshape(total, 128), features)
    mixed = mixed.T
    for k in range(3):
        grad_mix[32 * k : 32 * (k + 1), :] = sum(
            mixed[128 * k + 32 * t : 128 * k + 32 * (t + 1), 32 * t : 32 * (t + 1)]
            for t in range(4)
        )

    for copy in small_copies + big_copies + pass_copies:
        copy.wait_send()


def whole_in_kernel(
    series, starts, sensor_order, emb_src, emb_dst, start_proj, conv_weight, mix_weight, out_grad
):
    n = lax.axis_size("sensor")
    total = 48 * n
    vmem = pl.BlockSpec(memory_space=pltpu.VMEM)
    dma = pltpu.SemaphoreType.DMA
    return pl.pallas_call(
        lambda *refs: layer_kernel(n, *refs),
        out_shape=(
            jax.ShapeDtypeStruct((48, 384), bf16),
            jax.ShapeDtypeStruct((10, 48), f32),
            jax.ShapeDtypeStruct((10, 48), f32),
            jax.ShapeDtypeStruct((96, 32), f32),
        ),
        in_specs=[pl.BlockSpec(memory_space=pltpu.SMEM)] + [vmem] * 8,
        out_specs=(vmem,) * 4,
        scratch_shapes=[
            pltpu.VMEM((128, 128), f32),
            pltpu.VMEM((PIECE * n, 128), f32),
            pltpu.VMEM((QUARTERS, PIECE * n, 384), bf16),
            pltpu.VMEM((total, 128), bf16),
            pltpu.VMEM((total, 128), bf16),
            pltpu.VMEM((total, 128), f32),
            pltpu.VMEM((total, 128), bf16),
            pltpu.VMEM((total, 384), bf16),
            pltpu.VMEM((total, 384), bf16),
            pltpu.VMEM((total, total), bf16),
            pltpu.VMEM((total, 384), f32),
            pltpu.VMEM((total, 384), bf16),
            pltpu.VMEM((total, 384), f32),
            pltpu.VMEM((total, 384), bf16),
            pltpu.VMEM((total, 384), bf16),
            pltpu.VMEM((total, 384), bf16),
            pltpu.VMEM((total, 384), bf16),
            pltpu.VMEM((total, 128), f32),
            dma((n,)),
            dma((n,)),
            dma((n // 2,)),
            dma((n // 2,)),
            dma((n // 2,)),
            dma((n // 2,)),
        ],
        compiler_params=pltpu.CompilerParams(
            collective_id=0, has_side_effects=True, vmem_limit_bytes=48 * 2**20
        ),
    )(
        starts, series, sensor_order.reshape(1, -1), emb_src, emb_dst, start_proj, conv_weight,
        mix_weight, out_grad,
    )


def layer_on_device(*operands):
    if lax.axis_size("sensor") == 16 and operands[2].shape[0] == 48:
        return whole_in_kernel(*operands)
    return per_device(*operands)


def solution(mesh):
    placed = (
        P(None, ("groups", "sensor")),
        P("groups"),
        P(("groups", "sensor")),
        P(None, ("groups", "sensor")),
        P(None, ("groups", "sensor")),
        P(),
        P(),
        P(),
        P(("groups", "sensor"), None),
    )
    return jax.shard_map(
        layer_on_device,
        mesh=mesh,
        in_specs=placed,
        out_specs=(
            P(("groups", "sensor"), None),
            P(None, ("groups", "sensor")),
            P(None, ("groups", "sensor")),
            P("groups", None),
        ),
        check_vma=False,
    )
```

```python
import math

import jax
import jax.numpy as jnp
from jax import lax
from jax.experimental import pallas as pl
from jax.experimental.pallas import tpu as pltpu
from jax.sharding import PartitionSpec as P

STEPS = 12


highest = lax.Precision.HIGHEST


def front(readings, start_proj, conv_weight):
    sensors_here = readings.shape[0]
    channels = start_proj.shape[1]
    padded = jnp.concatenate(
        [jnp.zeros(readings.shape[:-1] + (1,), jnp.float32), readings], axis=-1
    )
    inputs = (padded[..., None] * start_proj[0] + start_proj[1]).astype(jnp.bfloat16)
    paired = jnp.concatenate([inputs[:, :, :-1, :], inputs[:, :, 1:, :]], axis=-1).reshape(
        -1, 2 * channels
    )
    gate_terms = jnp.dot(paired, conv_weight, preferred_element_type=jnp.float32)
    hidden = (jnp.tanh(gate_terms[:, :channels]) * jax.nn.sigmoid(gate_terms[:, channels:])).astype(
        jnp.bfloat16
    )
    return (hidden.reshape(sensors_here, -1), inputs[:, :, 1:, :].reshape(sensors_here, -1))


def mixing(residual, hidden, diffused, second, mix_weight):
    channels = mix_weight.shape[1]
    stacked = jnp.concatenate(
        [member.reshape(-1, channels) for member in (hidden, diffused, second)], axis=1
    )
    summed = residual.reshape(-1, channels).astype(jnp.float32) + jnp.dot(
        stacked, mix_weight, preferred_element_type=jnp.float32
    )
    return (summed.astype(jnp.bfloat16).reshape(hidden.shape[0], -1), stacked)


def channel_grads(out_grad, mix_weight):
    channels = mix_weight.shape[1]
    row_count = out_grad.shape[0]
    flat_grad = out_grad.reshape(-1, channels)
    dims = (((1,), (1,)), ((), ()))
    grad_once = lax.dot_general(
        flat_grad, mix_weight[channels : 2 * channels], dims, preferred_element_type=jnp.float32
    )
    grad_twice = lax.dot_general(
        flat_grad, mix_weight[2 * channels :], dims, preferred_element_type=jnp.float32
    )
    return (
        grad_once.astype(jnp.bfloat16).reshape(row_count, -1),
        grad_twice.astype(jnp.bfloat16).reshape(row_count, -1),
    )


def tile_probs(rows_emb, cols_emb, row_max, row_total):
    scores = jnp.einsum("ei,ej->ij", rows_emb, cols_emb, precision=highest)
    shares = jnp.exp(jnp.maximum(scores, 0.0) - row_max[:, None]) / row_total[:, None]
    return (scores, shares)


def pair_dot(left, right):
    return lax.dot_general(
        left, right, (((1,), (1,)), ((), ())), preferred_element_type=jnp.float32
    )


def in_blocks(step_fn, status, members, axis_dim):
    amount = members[0].shape[axis_dim]
    span_size = math.gcd(amount, 512)

    def advance(position, current):
        opening = position * span_size
        sliced = tuple(
            (lax.dynamic_slice_in_dim(member, opening, span_size, axis_dim) for member in members)
        )
        return step_fn(current, sliced, opening)

    return lax.fori_loop(0, amount // span_size, advance, status)


def score_grads(status, emb_src, cols_dst, offset, scores, shares, dweights):
    grad_rows, grad_cols = status
    dscore = jnp.where(scores > 0.0, shares * dweights, 0.0)
    grad_rows = grad_rows + jnp.einsum("ej,ij->ei", cols_dst, dscore, precision=highest)
    span_size = dscore.shape[1]
    current = lax.dynamic_slice_in_dim(grad_cols, offset, span_size, 1)
    added = current + jnp.einsum("ei,ij->ej", emb_src, dscore, precision=highest)
    return (grad_rows, lax.dynamic_update_slice_in_dim(grad_cols, added, offset, 1))


def per_device(
    series, starts, sensor_order, emb_src, emb_dst, start_proj, conv_weight, mix_weight, out_grad
):
    local_rows = sensor_order.shape[0]
    embed_dim = emb_src.shape[0]
    channels = start_proj.shape[1]
    all_rows = local_rows * lax.axis_size("sensor")
    windows = jax.vmap(lambda first_step: lax.dynamic_slice_in_dim(series, first_step, STEPS, 0))(
        starts
    )
    flat_windows = windows.reshape(-1, local_rows)
    window_rows = flat_windows.shape[0]

    def pick_step(status, members, offset):
        readings_sum, dst_all = status
        block_windows, block_dst = members
        span_size = block_windows.shape[1]
        onehot = (sensor_order[:, None] == offset + lax.iota(jnp.int32, span_size)[None, :]).astype(
            jnp.float32
        )
        readings_sum = readings_sum + jnp.einsum(
            "wj,pj->wp", block_windows, onehot, precision=highest
        )
        return (readings_sum, lax.dynamic_update_slice_in_dim(dst_all, block_dst, offset, 1))

    readings_sum, dst_all = in_blocks(
        pick_step,
        (
            jnp.zeros((window_rows, local_rows), jnp.float32),
            jnp.zeros((embed_dim, all_rows), jnp.float32),
        ),
        (
            lax.all_gather(flat_windows, "sensor", axis=1, tiled=True),
            lax.all_gather(emb_dst, "sensor", axis=1, tiled=True),
        ),
        1,
    )
    readings = readings_sum.T.reshape(local_rows, -1, STEPS)
    hidden, residual = front(readings, start_proj, conv_weight)
    feat_cols = hidden.shape[1]
    span_all = math.gcd(all_rows, 512)

    def stat_step(position, current):
        best_score, summed = current
        cols_dst = lax.dynamic_slice_in_dim(dst_all, position * span_all, span_all, 1)
        scores = jnp.maximum(jnp.einsum("ei,ej->ij", emb_src, cols_dst, precision=highest), 0.0)
        new_best = jnp.maximum(best_score, jnp.max(scores, axis=1))
        summed = summed * jnp.exp(best_score - new_best) + jnp.sum(
            jnp.exp(scores - new_best[:, None]), axis=1
        )
        return (new_best, summed)

    row_max, row_total = lax.fori_loop(
        0,
        all_rows // span_all,
        stat_step,
        (jnp.zeros((local_rows,), jnp.float32), jnp.zeros((local_rows,), jnp.float32)),
    )
    grad_once, grad_twice = channel_grads(out_grad, mix_weight)

    def spread_step(status, members, offset):
        block_feat = members[0]
        cols_dst = lax.dynamic_slice_in_dim(dst_all, offset, block_feat.shape[0], 1)
        scores, shares = tile_probs(emb_src, cols_dst, row_max, row_total)
        return status + jnp.dot(
            shares.astype(jnp.bfloat16), block_feat, preferred_element_type=jnp.float32
        )

    first_init = jnp.zeros((local_rows, feat_cols), jnp.float32)
    first_result = in_blocks(
        spread_step, first_init, (lax.all_gather(hidden, "sensor", axis=0, tiled=True),), 0
    )
    diffused = first_result.astype(jnp.bfloat16)

    def plain_step(status, members, offset):
        accumulated, grad_rows, grad_cols = status
        return (spread_step(accumulated, members, offset), grad_rows, grad_cols)

    second_init = (
        jnp.zeros((local_rows, feat_cols), jnp.float32),
        jnp.zeros((embed_dim, local_rows), jnp.float32),
        jnp.zeros((embed_dim, all_rows), jnp.float32),
    )
    second_result = in_blocks(
        plain_step, second_init, (lax.all_gather(diffused, "sensor", axis=0, tiled=True),), 0
    )
    second_full, grad_rows, grad_cols = second_result
    second = second_full.astype(jnp.bfloat16)
    layer_out, stacked = mixing(residual, hidden, diffused, second, mix_weight)
    mix_part = lax.dot_general(
        stacked,
        out_grad.reshape(-1, channels),
        (((0,), (0,)), ((), ())),
        preferred_element_type=jnp.float32,
    )
    span_size = math.gcd(lax.axis_size("sensor") * local_rows, 512)

    def piece_term(position):
        cols_dst = lax.dynamic_slice_in_dim(dst_all, position * span_size, span_size, 1)
        scores, shares = tile_probs(emb_src, cols_dst, row_max, row_total)
        return lax.dot_general(
            shares.astype(jnp.bfloat16),
            grad_twice,
            (((0,), (0,)), ((), ())),
            preferred_element_type=jnp.float32,
        )

    adjoint_sum = lax.psum_scatter(
        lax.map(
            piece_term,
            jnp.arange(lax.axis_size("sensor") * local_rows // span_size, dtype=jnp.int32),
        ).reshape(lax.axis_size("sensor") * local_rows, -1),
        "sensor",
        scatter_dimension=0,
        tiled=True,
    )
    carried = (grad_once.astype(jnp.float32) + adjoint_sum).astype(jnp.bfloat16)
    row_delta = jnp.sum(
        grad_twice.astype(jnp.float32) * second_full + carried.astype(jnp.float32) * first_result,
        axis=1,
    )

    def pair_step(status, members, offset):
        block_hidden, block_diff = members
        cols_dst = lax.dynamic_slice_in_dim(dst_all, offset, block_hidden.shape[0], 1)
        scores, shares = tile_probs(emb_src, cols_dst, row_max, row_total)
        dweights = (
            pair_dot(grad_twice, block_diff) + pair_dot(carried, block_hidden) - row_delta[:, None]
        )
        return score_grads(status, emb_src, cols_dst, offset, scores, shares, dweights)

    grad_rows, grad_cols = in_blocks(
        pair_step,
        (grad_rows, grad_cols),
        (
            lax.all_gather(hidden, "sensor", axis=0, tiled=True),
            lax.all_gather(diffused, "sensor", axis=0, tiled=True),
        ),
        0,
    )
    grad_dst = lax.psum_scatter(grad_cols, "sensor", scatter_dimension=1, tiled=True)
    grad_mix = lax.psum(mix_part, "sensor")
    return (layer_out, grad_rows, grad_dst, grad_mix)


PIECE = 16
QUARTERS = 3
NT = (((1,), (1,)), ((), ()))
TN = (((0,), (0,)), ((), ()))
f32 = jnp.float32
bf16 = jnp.bfloat16


def iota(shape, dim):
    return lax.broadcasted_iota(jnp.int32, shape, dim)


def ones_where(mask):
    return jnp.where(mask, 1.0, 0.0).astype(bf16)


def nn(left, right):
    return jnp.dot(left, right, preferred_element_type=f32)


def nt(left, right):
    return lax.dot_general(left, right, NT, preferred_element_type=f32)


def tn(left, right):
    return lax.dot_general(left, right, TN, preferred_element_type=f32)


def halves(value):
    high = value.astype(bf16)
    return high, (value - high.astype(f32)).astype(bf16)


def thirds(value):
    high, middle = halves(value)
    return high, middle, (value - high.astype(f32) - middle.astype(f32)).astype(bf16)


def selection(q):
    col = iota((1, 384), 1)
    tile, lane = col >> 7, col & 127
    u, e = lane >> 4, lane & 15
    left = jnp.where((u == 2) | (u == 5), 1, jnp.where(u == 4, 2, 0)) * 128 + e
    right = jnp.where((u == 1) | (u == 5), 1, jnp.where(u == 3, 2, 0)) * 128 + e + 10
    window = u * 128 + e + 20
    wanted = jnp.where(tile == 0, left, jnp.where(tile == 1, right, window))
    blocks, width = jnp.where(tile == 2, 3, 6), jnp.where(tile == 2, 12, 10)
    wanted = jnp.where((u < blocks) & (e < width), wanted + 40 * q, -1)
    number = jnp.where(col == 320, 32 + 40 * q, -1)
    row = iota((384, 384), 0)
    return ones_where((row == wanted) | ((row & 127) == number))


def gather_kernel(
    n, starts, series_in, order_in, src_in, dst_in, proj_in, conv_in, mix_in, out_grad_in,
    grads, left_emb, right_emb, hidden, residual, diffused, second, twice, carried, stats, mix_out,
    series, order, src, dst, start_proj, conv, mix, out_grad,
    packed, small, window_f, window_b, adj, diff_full, second_full, once,
    load_sem, small_send, small_recv, big_send, big_recv, pass_send, pass_recv,
):
    loads = [
        pltpu.make_async_copy(source, target, load_sem.at[at])
        for at, (source, target) in enumerate(
            [
                (series_in, series), (order_in, order), (src_in, src), (dst_in, dst),
                (out_grad_in, out_grad), (conv_in, conv), (mix_in, mix), (proj_in, start_proj),
            ]
        )
    ]
    for load in loads:
        load.start()
    me = lax.axis_index("sensor")
    rows_q = PIECE * n
    total = QUARTERS * rows_q
    barrier = pltpu.get_barrier_semaphore()
    for k in range(1, n):
        pl.semaphore_signal(
            barrier, inc=1, device_id={"sensor": lax.rem(me + k, n)},
            device_id_type=pl.DeviceIdType.MESH,
        )
    mine = pl.multiple_of(me * PIECE, PIECE)

    wanted = ones_where(iota((16, series.shape[1]), 1) == iota((16, series.shape[1]), 0) + starts[0])
    for load in loads[:4]:
        load.wait()
    window = sum(nt(wanted, part) for part in thirds(series[...]))[0:STEPS, :]
    block = jnp.concatenate(
        [src[...], dst[...], window, order[...].astype(f32), jnp.zeros((7, 48), f32)], axis=0
    )
    packed[...] = jnp.zeros_like(packed)
    for q in range(QUARTERS):
        packed[40 * q : 40 * q + 40, 0:PIECE] = block[:, PIECE * q : PIECE * (q + 1)]
    small[pl.ds(mine, PIECE), :] = packed[...].T[0:PIECE, :]
    loads[4].wait()
    for q in range(QUARTERS):
        grads[q, pl.ds(mine, PIECE), :] = out_grad[PIECE * q : PIECE * (q + 1), :]

    pl.semaphore_wait(barrier, n - 1)

    def remote(where, send, recv, peer):
        return pltpu.make_async_remote_copy(
            src_ref=where, dst_ref=where, send_sem=send, recv_sem=recv,
            device_id={"sensor": peer}, device_id_type=pl.DeviceIdType.MESH,
        )

    small_copies = []
    for k in range(1, n):
        copy = remote(
            small.at[pl.ds(mine, PIECE), :], small_send.at[k], small_recv.at[k],
            lax.rem(me + k, n),
        )
        copy.start()
        small_copies.append(copy)
    sibling = me + 1 - 2 * lax.rem(me, 2)
    big_copies = []
    for k in range(n // 2):
        copy = remote(
            grads.at[:, pl.ds(mine, PIECE), :], big_send.at[k], big_recv.at[k],
            sibling if k == 0 else lax.rem(me + 2 * k, n),
        )
        copy.start()
        big_copies.append(copy)

    for load in loads[5:]:
        load.wait()

    spread = ones_where(iota((256, 64), 1) == (iota((256, 64), 0) >> 7) * 32 + (iota((256, 64), 0) & 31))
    gather = ones_where(iota((64, 256), 0) == (iota((64, 256), 1) >> 7) * 32 + (iota((64, 256), 1) & 31))
    conv_big = nn(nn(spread, conv[...]).astype(bf16), gather)
    conv_big = jnp.where(
        ((iota((256, 256), 0) & 127) >> 5) == ((iota((256, 256), 1) & 127) >> 5), conv_big, 0.0
    ).astype(bf16)
    spread = ones_where(iota((384, 96), 1) == (iota((384, 96), 0) >> 7) * 32 + (iota((384, 96), 0) & 31))
    gather = ones_where(iota((32, 128), 0) == (iota((32, 128), 1) & 31))
    mix_big = nn(nt(spread, mix[...]).astype(bf16), gather)
    mix_big = jnp.where(
        ((iota((384, 128), 0) & 127) >> 5) == (iota((384, 128), 1) >> 5), mix_big, 0.0
    ).astype(bf16)
    mix_out[...] = mix_big
    proj = jnp.concatenate([start_proj[...]] * 4, axis=1)
    weight, bias = proj[0:1, :], proj[1:2, :]
    at = iota((128, 768), 0)
    col = iota((128, 768), 1)
    step = jnp.where(col < 384, (col >> 5) - 1, (col - 384) >> 5)
    expand = ones_where(((at & 15) == step) & (at < 48))
    numbers = jnp.concatenate(
        [
            48 * (iota((1, rows_q), 1) >> 4) + PIECE * q + (iota((1, rows_q), 1) & 15)
            for q in range(QUARTERS)
        ],
        axis=1,
    ).astype(f32)

    for copy in small_copies:
        copy.wait_recv()

    parts = jnp.concatenate(thirds(small[...]), axis=1)
    for q in range(QUARTERS):
        taken = nn(parts, selection(q))
        rows = slice(q * rows_q, (q + 1) * rows_q)
        left_emb[rows, :] = taken[:, 0:128].astype(bf16)
        right_emb[rows, :] = taken[:, 128:256].astype(bf16)
        window_f[rows, :] = taken[:, 256:384]
        window_b[rows, :] = taken[:, 256:384].astype(bf16)

    def chunk(q):
        return pl.ds(pl.multiple_of(q * rows_q, rows_q), rows_q)

    def front_step(q, carry):
        rows = chunk(q)
        onehot = ones_where(window_f[rows, 64:65] == numbers)
        picked = nn(onehot, window_b[...]).astype(bf16)
        wide = nn(picked, expand)
        for b in range(3):
            lanes = slice(128 * b, 128 * (b + 1))
            before = (wide[:, 128 * b : 128 * (b + 1)] * weight + bias).astype(bf16)
            after = (wide[:, 384 + 128 * b : 512 + 128 * b] * weight + bias).astype(bf16)
            residual[rows, lanes] = after
            terms = nn(jnp.concatenate([before, after], axis=1), conv_big)
            gated = jnp.tanh(terms[:, :128]) * (0.5 * jnp.tanh(0.5 * terms[:, 128:]) + 0.5)
            hidden[rows, lanes] = gated.astype(bf16)
        return carry

    lax.fori_loop(0, QUARTERS, front_step, 0)

    def first_step(q, carry):
        rows = chunk(q)
        positive = jnp.maximum(nt(left_emb[rows, :], right_emb[...]), 0.0)
        top = jnp.max(positive, axis=1, keepdims=True)
        terms = jnp.exp(positive - top)
        inverse = 1.0 / jnp.sum(terms, axis=1, keepdims=True)
        weights = (terms * inverse).astype(bf16)
        adj[rows, :] = weights
        stats[rows, 0:1] = top
        stats[rows, 1:2] = inverse
        result = nn(weights, hidden[...])
        diff_full[rows, :] = result
        diffused[rows, :] = result.astype(bf16)
        return carry

    lax.fori_loop(0, QUARTERS, first_step, 0)

    pass_copies = []
    for k in range(1, n // 2):
        big_copies[k].wait_recv()
        origin = pl.multiple_of(lax.rem(me + n - 2 * k, n) * PIECE, PIECE)
        copy = remote(
            grads.at[:, pl.ds(origin, PIECE), :], pass_send.at[k], pass_recv.at[k], sibling
        )
        copy.start()
        pass_copies.append(copy)

    def second_step(q, carry):
        rows = chunk(q)
        result = nn(adj[rows, :], diffused[...])
        second_full[rows, :] = result
        second[rows, :] = result.astype(bf16)
        return carry

    lax.fori_loop(0, QUARTERS, second_step, 0)

    big_copies[0].wait_recv()
    for copy in pass_copies:
        copy.wait_recv()

    def channel_step(q, carry):
        rows = chunk(q)
        given = grads[q]
        for b in range(3):
            lanes = slice(128 * b, 128 * (b + 1))
            both = nt(given[:, lanes], mix_big[128:384, :]).astype(bf16)
            once[rows, lanes] = both[:, :128]
            twice[rows, lanes] = both[:, 128:]
        return carry

    lax.fori_loop(0, QUARTERS, channel_step, 0)

    def adjoint_step(q, carry):
        rows = chunk(q)
        back = tn(adj[:, rows], twice[...])
        total_grad = (once[rows, :].astype(f32) + back).astype(bf16)
        carried[rows, :] = total_grad
        delta = twice[rows, :].astype(f32) * second_full[rows, :] + total_grad.astype(
            f32
        ) * diff_full[rows, :]
        stats[rows, 2:3] = jnp.sum(delta, axis=1, keepdims=True)
        return carry

    lax.fori_loop(0, QUARTERS, adjoint_step, 0)

    for copy in small_copies + big_copies + pass_copies:
        copy.wait_send()


def finish_kernel(
    n, grads, left_emb, right_emb, hidden, residual, diffused, second, twice, carried, stats, mix_big,
    layer_out_to, grad_src_to, grad_dst_to, grad_mix_to,
    layer_out, grad_src, grad_dst, grad_mix, store_sem,
):
    me = lax.axis_index("sensor")
    rows_q = PIECE * n
    total = QUARTERS * rows_q
    stores = [
        pltpu.make_async_copy(source, target, store_sem.at[at])
        for at, (source, target) in enumerate(
            [
                (layer_out, layer_out_to), (grad_mix, grad_mix_to),
                (grad_src, grad_src_to), (grad_dst, grad_dst_to),
            ]
        )
    ]

    def own(ref):
        return jnp.concatenate(
            [
                ref[pl.ds(pl.multiple_of(q * rows_q + me * PIECE, PIECE), PIECE), :]
                for q in range(QUARTERS)
            ],
            axis=0,
        )

    own_hidden, own_diff, own_second = own(hidden), own(diffused), own(second)
    own_left, own_right, own_stats = own(left_emb), own(right_emb), own(stats)
    own_residual = own(residual)
    for b in range(3):
        lanes = slice(128 * b, 128 * (b + 1))
        features = jnp.concatenate(
            [own_hidden[:, lanes], own_diff[:, lanes], own_second[:, lanes]], axis=1
        )
        layer_out[:, lanes] = (own_residual[:, lanes].astype(f32) + nn(features, mix_big[...])).astype(
            bf16
        )

    stores[0].start()

    mixed = jnp.zeros((128, 384), f32)
    for b in range(3):
        lanes = slice(128 * b, 128 * (b + 1))
        features = jnp.concatenate([hidden[:, lanes], diffused[:, lanes], second[:, lanes]], axis=1)
        mixed = mixed + tn(grads[:, :, lanes].reshape(total, 128), features)
    for k in range(3):
        grad_mix[:, 32 * k : 32 * (k + 1)] = sum(
            mixed[32 * t : 32 * (t + 1), 128 * k + 32 * t : 128 * k + 32 * (t + 1)]
            for t in range(4)
        )
    stores[1].start()

    def score_grad(scores, stat, products):
        shares = jnp.exp(jnp.maximum(scores, 0.0) - stat[:, 0:1]) * stat[:, 1:2]
        return halves(jnp.where(scores > 0.0, shares * (products - stat[:, 2:3]), 0.0))

    high, low = score_grad(
        nt(own_left, right_emb[...]),
        own_stats,
        nt(own(twice), diffused[...]) + nt(own(carried), hidden[...]),
    )
    summed = (nn(high, right_emb[...]) + nn(low, right_emb[...])).T
    grad_src[...] = summed[0:10, :] + summed[16:26, :] + summed[48:58, :]
    stores[2].start()

    high, low = score_grad(
        nt(left_emb[...], own_right),
        stats[...],
        nt(twice[...], own_diff) + nt(carried[...], own_hidden),
    )
    summed = tn(left_emb[...], high) + tn(left_emb[...], low)
    grad_dst[...] = summed[0:10, :] + summed[32:42, :] + summed[64:74, :]
    stores[3].start()
    for store in stores:
        store.wait()


def whole_in_kernel(
    series, starts, sensor_order, emb_src, emb_dst, start_proj, conv_weight, mix_weight, out_grad
):
    n = lax.axis_size("sensor")
    total = 48 * n
    vmem = pl.BlockSpec(memory_space=pltpu.VMEM)
    anywhere = pl.BlockSpec(memory_space=pltpu.HBM)
    dma = pltpu.SemaphoreType.DMA
    wide = jax.ShapeDtypeStruct((total, 384), bf16)
    lane = jax.ShapeDtypeStruct((total, 128), bf16)
    operands = (
        series.T, sensor_order.reshape(1, -1), emb_src, emb_dst, start_proj, conv_weight,
        mix_weight.T, out_grad,
    )
    operands = tuple(pltpu.with_memory_space_constraint(operand, pltpu.HBM) for operand in operands)
    held = pl.pallas_call(
        lambda *refs: gather_kernel(n, *refs),
        out_shape=(
            jax.ShapeDtypeStruct((QUARTERS, PIECE * n, 384), bf16),
            lane, lane, wide, wide, wide, wide, wide, wide,
            jax.ShapeDtypeStruct((total, 128), f32),
            jax.ShapeDtypeStruct((384, 128), bf16),
        ),
        in_specs=[pl.BlockSpec(memory_space=pltpu.SMEM)] + [anywhere] * 8,
        out_specs=(vmem,) * 11,
        scratch_shapes=[pltpu.VMEM(operand.shape, operand.dtype) for operand in operands]
        + [
            pltpu.VMEM((128, 128), f32),
            pltpu.VMEM((PIECE * n, 128), f32),
            pltpu.VMEM((total, 128), f32),
            pltpu.VMEM((total, 128), bf16),
            pltpu.VMEM((total, total), bf16),
            pltpu.VMEM((total, 384), f32),
            pltpu.VMEM((total, 384), f32),
            pltpu.VMEM((total, 384), bf16),
            dma((8,)),
            dma((n,)),
            dma((n,)),
            dma((n // 2,)),
            dma((n // 2,)),
            dma((n // 2,)),
            dma((n // 2,)),
        ],
        compiler_params=pltpu.CompilerParams(
            collective_id=0, has_side_effects=True, vmem_limit_bytes=32 * 2**20
        ),
    )(starts, *operands)
    outs = (
        jax.ShapeDtypeStruct((48, 384), bf16),
        jax.ShapeDtypeStruct((10, 48), f32),
        jax.ShapeDtypeStruct((10, 48), f32),
        jax.ShapeDtypeStruct((32, 96), f32),
    )
    layer_out, grad_src, grad_dst, grad_mix = pl.pallas_call(
        lambda *refs: finish_kernel(n, *refs),
        out_shape=outs,
        in_specs=[vmem] * 11,
        out_specs=(anywhere,) * 4,
        scratch_shapes=[pltpu.VMEM(out.shape, out.dtype) for out in outs] + [dma((4,))],
        compiler_params=pltpu.CompilerParams(vmem_limit_bytes=32 * 2**20),
    )(*held)
    return layer_out, grad_src, grad_dst, grad_mix.T


def layer_on_device(*operands):
    if lax.axis_size("sensor") == 16 and operands[2].shape[0] == 48:
        return whole_in_kernel(*operands)
    return per_device(*operands)


def solution(mesh):
    placed = (
        P(None, ("groups", "sensor")),
        P("groups"),
        P(("groups", "sensor")),
        P(None, ("groups", "sensor")),
        P(None, ("groups", "sensor")),
        P(),
        P(),
        P(),
        P(("groups", "sensor"), None),
    )
    return jax.shard_map(
        layer_on_device,
        mesh=mesh,
        in_specs=placed,
        out_specs=(
            P(("groups", "sensor"), None),
            P(None, ("groups", "sensor")),
            P(None, ("groups", "sensor")),
            P("groups", None),
        ),
        check_vma=False,
    )
```

```python
import math

import jax
import jax.numpy as jnp
from jax import lax
from jax.experimental import pallas as pl
from jax.experimental.pallas import tpu as pltpu
from jax.sharding import PartitionSpec as P

STEPS = 12


highest = lax.Precision.HIGHEST


def front(readings, start_proj, conv_weight):
    sensors_here = readings.shape[0]
    channels = start_proj.shape[1]
    padded = jnp.concatenate(
        [jnp.zeros(readings.shape[:-1] + (1,), jnp.float32), readings], axis=-1
    )
    inputs = (padded[..., None] * start_proj[0] + start_proj[1]).astype(jnp.bfloat16)
    paired = jnp.concatenate([inputs[:, :, :-1, :], inputs[:, :, 1:, :]], axis=-1).reshape(
        -1, 2 * channels
    )
    gate_terms = jnp.dot(paired, conv_weight, preferred_element_type=jnp.float32)
    hidden = (jnp.tanh(gate_terms[:, :channels]) * jax.nn.sigmoid(gate_terms[:, channels:])).astype(
        jnp.bfloat16
    )
    return (hidden.reshape(sensors_here, -1), inputs[:, :, 1:, :].reshape(sensors_here, -1))


def mixing(residual, hidden, diffused, second, mix_weight):
    channels = mix_weight.shape[1]
    stacked = jnp.concatenate(
        [member.reshape(-1, channels) for member in (hidden, diffused, second)], axis=1
    )
    summed = residual.reshape(-1, channels).astype(jnp.float32) + jnp.dot(
        stacked, mix_weight, preferred_element_type=jnp.float32
    )
    return (summed.astype(jnp.bfloat16).reshape(hidden.shape[0], -1), stacked)


def channel_grads(out_grad, mix_weight):
    channels = mix_weight.shape[1]
    row_count = out_grad.shape[0]
    flat_grad = out_grad.reshape(-1, channels)
    dims = (((1,), (1,)), ((), ()))
    grad_once = lax.dot_general(
        flat_grad, mix_weight[channels : 2 * channels], dims, preferred_element_type=jnp.float32
    )
    grad_twice = lax.dot_general(
        flat_grad, mix_weight[2 * channels :], dims, preferred_element_type=jnp.float32
    )
    return (
        grad_once.astype(jnp.bfloat16).reshape(row_count, -1),
        grad_twice.astype(jnp.bfloat16).reshape(row_count, -1),
    )


def tile_probs(rows_emb, cols_emb, row_max, row_total):
    scores = jnp.einsum("ei,ej->ij", rows_emb, cols_emb, precision=highest)
    shares = jnp.exp(jnp.maximum(scores, 0.0) - row_max[:, None]) / row_total[:, None]
    return (scores, shares)


def pair_dot(left, right):
    return lax.dot_general(
        left, right, (((1,), (1,)), ((), ())), preferred_element_type=jnp.float32
    )


def in_blocks(step_fn, status, members, axis_dim):
    amount = members[0].shape[axis_dim]
    span_size = math.gcd(amount, 512)

    def advance(position, current):
        opening = position * span_size
        sliced = tuple(
            (lax.dynamic_slice_in_dim(member, opening, span_size, axis_dim) for member in members)
        )
        return step_fn(current, sliced, opening)

    return lax.fori_loop(0, amount // span_size, advance, status)


def score_grads(status, emb_src, cols_dst, offset, scores, shares, dweights):
    grad_rows, grad_cols = status
    dscore = jnp.where(scores > 0.0, shares * dweights, 0.0)
    grad_rows = grad_rows + jnp.einsum("ej,ij->ei", cols_dst, dscore, precision=highest)
    span_size = dscore.shape[1]
    current = lax.dynamic_slice_in_dim(grad_cols, offset, span_size, 1)
    added = current + jnp.einsum("ei,ij->ej", emb_src, dscore, precision=highest)
    return (grad_rows, lax.dynamic_update_slice_in_dim(grad_cols, added, offset, 1))


def per_device(
    series, starts, sensor_order, emb_src, emb_dst, start_proj, conv_weight, mix_weight, out_grad
):
    local_rows = sensor_order.shape[0]
    embed_dim = emb_src.shape[0]
    channels = start_proj.shape[1]
    all_rows = local_rows * lax.axis_size("sensor")
    windows = jax.vmap(lambda first_step: lax.dynamic_slice_in_dim(series, first_step, STEPS, 0))(
        starts
    )
    flat_windows = windows.reshape(-1, local_rows)
    window_rows = flat_windows.shape[0]

    def pick_step(status, members, offset):
        readings_sum, dst_all = status
        block_windows, block_dst = members
        span_size = block_windows.shape[1]
        onehot = (sensor_order[:, None] == offset + lax.iota(jnp.int32, span_size)[None, :]).astype(
            jnp.float32
        )
        readings_sum = readings_sum + jnp.einsum(
            "wj,pj->wp", block_windows, onehot, precision=highest
        )
        return (readings_sum, lax.dynamic_update_slice_in_dim(dst_all, block_dst, offset, 1))

    readings_sum, dst_all = in_blocks(
        pick_step,
        (
            jnp.zeros((window_rows, local_rows), jnp.float32),
            jnp.zeros((embed_dim, all_rows), jnp.float32),
        ),
        (
            lax.all_gather(flat_windows, "sensor", axis=1, tiled=True),
            lax.all_gather(emb_dst, "sensor", axis=1, tiled=True),
        ),
        1,
    )
    readings = readings_sum.T.reshape(local_rows, -1, STEPS)
    hidden, residual = front(readings, start_proj, conv_weight)
    feat_cols = hidden.shape[1]
    span_all = math.gcd(all_rows, 512)

    def stat_step(position, current):
        best_score, summed = current
        cols_dst = lax.dynamic_slice_in_dim(dst_all, position * span_all, span_all, 1)
        scores = jnp.maximum(jnp.einsum("ei,ej->ij", emb_src, cols_dst, precision=highest), 0.0)
        new_best = jnp.maximum(best_score, jnp.max(scores, axis=1))
        summed = summed * jnp.exp(best_score - new_best) + jnp.sum(
            jnp.exp(scores - new_best[:, None]), axis=1
        )
        return (new_best, summed)

    row_max, row_total = lax.fori_loop(
        0,
        all_rows // span_all,
        stat_step,
        (jnp.zeros((local_rows,), jnp.float32), jnp.zeros((local_rows,), jnp.float32)),
    )
    grad_once, grad_twice = channel_grads(out_grad, mix_weight)

    def spread_step(status, members, offset):
        block_feat = members[0]
        cols_dst = lax.dynamic_slice_in_dim(dst_all, offset, block_feat.shape[0], 1)
        scores, shares = tile_probs(emb_src, cols_dst, row_max, row_total)
        return status + jnp.dot(
            shares.astype(jnp.bfloat16), block_feat, preferred_element_type=jnp.float32
        )

    first_init = jnp.zeros((local_rows, feat_cols), jnp.float32)
    first_result = in_blocks(
        spread_step, first_init, (lax.all_gather(hidden, "sensor", axis=0, tiled=True),), 0
    )
    diffused = first_result.astype(jnp.bfloat16)

    def plain_step(status, members, offset):
        accumulated, grad_rows, grad_cols = status
        return (spread_step(accumulated, members, offset), grad_rows, grad_cols)

    second_init = (
        jnp.zeros((local_rows, feat_cols), jnp.float32),
        jnp.zeros((embed_dim, local_rows), jnp.float32),
        jnp.zeros((embed_dim, all_rows), jnp.float32),
    )
    second_result = in_blocks(
        plain_step, second_init, (lax.all_gather(diffused, "sensor", axis=0, tiled=True),), 0
    )
    second_full, grad_rows, grad_cols = second_result
    second = second_full.astype(jnp.bfloat16)
    layer_out, stacked = mixing(residual, hidden, diffused, second, mix_weight)
    mix_part = lax.dot_general(
        stacked,
        out_grad.reshape(-1, channels),
        (((0,), (0,)), ((), ())),
        preferred_element_type=jnp.float32,
    )
    span_size = math.gcd(lax.axis_size("sensor") * local_rows, 512)

    def piece_term(position):
        cols_dst = lax.dynamic_slice_in_dim(dst_all, position * span_size, span_size, 1)
        scores, shares = tile_probs(emb_src, cols_dst, row_max, row_total)
        return lax.dot_general(
            shares.astype(jnp.bfloat16),
            grad_twice,
            (((0,), (0,)), ((), ())),
            preferred_element_type=jnp.float32,
        )

    adjoint_sum = lax.psum_scatter(
        lax.map(
            piece_term,
            jnp.arange(lax.axis_size("sensor") * local_rows // span_size, dtype=jnp.int32),
        ).reshape(lax.axis_size("sensor") * local_rows, -1),
        "sensor",
        scatter_dimension=0,
        tiled=True,
    )
    carried = (grad_once.astype(jnp.float32) + adjoint_sum).astype(jnp.bfloat16)
    row_delta = jnp.sum(
        grad_twice.astype(jnp.float32) * second_full + carried.astype(jnp.float32) * first_result,
        axis=1,
    )

    def pair_step(status, members, offset):
        block_hidden, block_diff = members
        cols_dst = lax.dynamic_slice_in_dim(dst_all, offset, block_hidden.shape[0], 1)
        scores, shares = tile_probs(emb_src, cols_dst, row_max, row_total)
        dweights = (
            pair_dot(grad_twice, block_diff) + pair_dot(carried, block_hidden) - row_delta[:, None]
        )
        return score_grads(status, emb_src, cols_dst, offset, scores, shares, dweights)

    grad_rows, grad_cols = in_blocks(
        pair_step,
        (grad_rows, grad_cols),
        (
            lax.all_gather(hidden, "sensor", axis=0, tiled=True),
            lax.all_gather(diffused, "sensor", axis=0, tiled=True),
        ),
        0,
    )
    grad_dst = lax.psum_scatter(grad_cols, "sensor", scatter_dimension=1, tiled=True)
    grad_mix = lax.psum(mix_part, "sensor")
    return (layer_out, grad_rows, grad_dst, grad_mix)


PIECE = 16
QUARTERS = 3
NT = (((1,), (1,)), ((), ()))
TN = (((0,), (0,)), ((), ()))
f32 = jnp.float32
bf16 = jnp.bfloat16


def iota(shape, dim):
    return lax.broadcasted_iota(jnp.int32, shape, dim)


def ones_where(mask):
    return jnp.where(mask, 1.0, 0.0).astype(bf16)


def nn(left, right):
    return jnp.dot(left, right, preferred_element_type=f32)


def nt(left, right):
    return lax.dot_general(left, right, NT, preferred_element_type=f32)


def tn(left, right):
    return lax.dot_general(left, right, TN, preferred_element_type=f32)


def halves(value):
    high = value.astype(bf16)
    return high, (value - high.astype(f32)).astype(bf16)


def thirds(value):
    high, middle = halves(value)
    return high, middle, (value - high.astype(f32) - middle.astype(f32)).astype(bf16)


def selection(q):
    col = iota((1, 384), 1)
    tile, lane = col >> 7, col & 127
    u, e = lane >> 4, lane & 15
    left = jnp.where((u == 2) | (u == 5), 1, jnp.where(u == 4, 2, 0)) * 128 + e
    right = jnp.where((u == 1) | (u == 5), 1, jnp.where(u == 3, 2, 0)) * 128 + e + 10
    window = u * 128 + e + 20
    wanted = jnp.where(tile == 0, left, jnp.where(tile == 1, right, window))
    blocks, width = jnp.where(tile == 2, 3, 6), jnp.where(tile == 2, 12, 10)
    wanted = jnp.where((u < blocks) & (e < width), wanted + 40 * q, -1)
    number = jnp.where(col == 320, 32 + 40 * q, -1)
    row = iota((384, 384), 0)
    return ones_where((row == wanted) | ((row & 127) == number))


def gather_kernel(
    n, starts, series_in, order_in, src_in, dst_in, proj_in, conv_in, mix_in, out_grad_in,
    grads, left_emb, right_emb, hidden, residual, diffused, second, twice, carried, stats, mix_out,
    series, order, src, dst, start_proj, conv, mix, out_grad,
    packed, small, window_f, window_b, adj, diff_full, second_full, once,
    load_sem, small_send, small_recv, big_send, big_recv, pass_send, pass_recv,
):
    loads = [
        pltpu.make_async_copy(source, target, load_sem.at[at])
        for at, (source, target) in enumerate(
            [
                (series_in, series), (order_in, order), (src_in, src), (dst_in, dst),
                (out_grad_in, out_grad), (conv_in, conv), (mix_in, mix), (proj_in, start_proj),
            ]
        )
    ]
    for load in loads:
        load.start()
    me = lax.axis_index("sensor")
    rows_q = PIECE * n
    total = QUARTERS * rows_q
    barrier = pltpu.get_barrier_semaphore()
    for k in range(1, n):
        pl.semaphore_signal(
            barrier, inc=1, device_id={"sensor": lax.rem(me + k, n)},
            device_id_type=pl.DeviceIdType.MESH,
        )
    mine = pl.multiple_of(me * PIECE, PIECE)

    wanted = ones_where(iota((16, series.shape[1]), 1) == iota((16, series.shape[1]), 0) + starts[0])
    for load in loads[:4]:
        load.wait()
    window = sum(nt(wanted, part) for part in thirds(series[...]))[0:STEPS, :]
    block = jnp.concatenate(
        [src[...], dst[...], window, order[...].astype(f32), jnp.zeros((7, 48), f32)], axis=0
    )
    packed[...] = jnp.zeros_like(packed)
    for q in range(QUARTERS):
        packed[40 * q : 40 * q + 40, 0:PIECE] = block[:, PIECE * q : PIECE * (q + 1)]
    small[pl.ds(mine, PIECE), :] = packed[...].T[0:PIECE, :]
    loads[4].wait()
    for q in range(QUARTERS):
        grads[q, pl.ds(mine, PIECE), :] = out_grad[PIECE * q : PIECE * (q + 1), :]

    pl.semaphore_wait(barrier, n - 1)

    def remote(where, send, recv, peer):
        return pltpu.make_async_remote_copy(
            src_ref=where, dst_ref=where, send_sem=send, recv_sem=recv,
            device_id={"sensor": peer}, device_id_type=pl.DeviceIdType.MESH,
        )

    small_copies = []
    sibling = me + 1 - 2 * lax.rem(me, 2)
    for k in range(n // 2):
        copy = remote(
            small.at[pl.ds(mine, PIECE), :], small_send.at[k], small_recv.at[k],
            sibling if k == 0 else lax.rem(me + 2 * k, n),
        )
        copy.start()
        small_copies.append(copy)
    big_copies = []
    for k in range(n // 2):
        copy = remote(
            grads.at[:, pl.ds(mine, PIECE), :], big_send.at[k], big_recv.at[k],
            sibling if k == 0 else lax.rem(me + 2 * k, n),
        )
        copy.start()
        big_copies.append(copy)

    for load in loads[5:]:
        load.wait()

    spread = ones_where(iota((256, 64), 1) == (iota((256, 64), 0) >> 7) * 32 + (iota((256, 64), 0) & 31))
    gather = ones_where(iota((64, 256), 0) == (iota((64, 256), 1) >> 7) * 32 + (iota((64, 256), 1) & 31))
    conv_big = nn(nn(spread, conv[...]).astype(bf16), gather)
    conv_big = jnp.where(
        ((iota((256, 256), 0) & 127) >> 5) == ((iota((256, 256), 1) & 127) >> 5), conv_big, 0.0
    ).astype(bf16)
    spread = ones_where(iota((384, 96), 1) == (iota((384, 96), 0) >> 7) * 32 + (iota((384, 96), 0) & 31))
    gather = ones_where(iota((32, 128), 0) == (iota((32, 128), 1) & 31))
    mix_big = nn(nt(spread, mix[...]).astype(bf16), gather)
    mix_big = jnp.where(
        ((iota((384, 128), 0) & 127) >> 5) == (iota((384, 128), 1) >> 5), mix_big, 0.0
    ).astype(bf16)
    mix_out[...] = mix_big
    proj = jnp.concatenate([start_proj[...]] * 4, axis=1)
    weight, bias = proj[0:1, :], proj[1:2, :]
    at = iota((128, 768), 0)
    col = iota((128, 768), 1)
    step = jnp.where(col < 384, (col >> 5) - 1, (col - 384) >> 5)
    expand = ones_where(((at & 15) == step) & (at < 48))
    numbers = jnp.concatenate(
        [
            48 * (iota((1, rows_q), 1) >> 4) + PIECE * q + (iota((1, rows_q), 1) & 15)
            for q in range(QUARTERS)
        ],
        axis=1,
    ).astype(f32)

    chosen = [selection(q) for q in range(QUARTERS)]
    for k in range(1, n // 2):
        small_copies[k].wait_recv()
        origin = pl.multiple_of(lax.rem(me + n - 2 * k, n) * PIECE, PIECE)
        copy = remote(
            small.at[pl.ds(origin, PIECE), :],
            small_send.at[n // 2 + k],
            small_recv.at[n // 2 + k],
            sibling,
        )
        copy.start()
        small_copies.append(copy)
    small_copies[0].wait_recv()
    for copy in small_copies[n // 2 :]:
        copy.wait_recv()

    parts = jnp.concatenate(thirds(small[...]), axis=1)
    for q in range(QUARTERS):
        taken = nn(parts, chosen[q])
        rows = slice(q * rows_q, (q + 1) * rows_q)
        left_emb[rows, :] = taken[:, 0:128].astype(bf16)
        right_emb[rows, :] = taken[:, 128:256].astype(bf16)
        window_f[rows, :] = taken[:, 256:384]
        window_b[rows, :] = taken[:, 256:384].astype(bf16)

    def chunk(q):
        return pl.ds(pl.multiple_of(q * rows_q, rows_q), rows_q)

    def front_step(q, carry):
        rows = chunk(q)
        onehot = ones_where(window_f[rows, 64:65] == numbers)
        picked = nn(onehot, window_b[...]).astype(bf16)
        wide = nn(picked, expand)
        for b in range(3):
            lanes = slice(128 * b, 128 * (b + 1))
            before = (wide[:, 128 * b : 128 * (b + 1)] * weight + bias).astype(bf16)
            after = (wide[:, 384 + 128 * b : 512 + 128 * b] * weight + bias).astype(bf16)
            residual[rows, lanes] = after
            terms = nn(jnp.concatenate([before, after], axis=1), conv_big)
            gated = jnp.tanh(terms[:, :128]) * (0.5 * jnp.tanh(0.5 * terms[:, 128:]) + 0.5)
            hidden[rows, lanes] = gated.astype(bf16)
        return carry

    lax.fori_loop(0, QUARTERS, front_step, 0, unroll=True)

    def first_step(q, carry):
        rows = chunk(q)
        positive = jnp.maximum(nt(left_emb[rows, :], right_emb[...]), 0.0)
        top = jnp.max(positive, axis=1, keepdims=True)
        terms = jnp.exp(positive - top)
        inverse = 1.0 / jnp.sum(terms, axis=1, keepdims=True)
        weights = (terms * inverse).astype(bf16)
        adj[rows, :] = weights
        stats[rows, 0:1] = top
        stats[rows, 1:2] = inverse
        result = nn(weights, hidden[...])
        diff_full[rows, :] = result
        diffused[rows, :] = result.astype(bf16)
        return carry

    lax.fori_loop(0, QUARTERS, first_step, 0, unroll=True)

    pass_copies = []
    for k in range(1, n // 2):
        big_copies[k].wait_recv()
        origin = pl.multiple_of(lax.rem(me + n - 2 * k, n) * PIECE, PIECE)
        copy = remote(
            grads.at[:, pl.ds(origin, PIECE), :], pass_send.at[k], pass_recv.at[k], sibling
        )
        copy.start()
        pass_copies.append(copy)

    def second_step(q, carry):
        rows = chunk(q)
        result = nn(adj[rows, :], diffused[...])
        second_full[rows, :] = result
        second[rows, :] = result.astype(bf16)
        return carry

    lax.fori_loop(0, QUARTERS, second_step, 0, unroll=True)

    big_copies[0].wait_recv()
    for copy in pass_copies:
        copy.wait_recv()

    def channel_step(q, carry):
        rows = chunk(q)
        given = grads[q]
        for b in range(3):
            lanes = slice(128 * b, 128 * (b + 1))
            both = nt(given[:, lanes], mix_big[128:384, :]).astype(bf16)
            once[rows, lanes] = both[:, :128]
            twice[rows, lanes] = both[:, 128:]
        return carry

    lax.fori_loop(0, QUARTERS, channel_step, 0, unroll=True)

    def adjoint_step(q, carry):
        rows = chunk(q)
        back = tn(adj[:, rows], twice[...])
        total_grad = (once[rows, :].astype(f32) + back).astype(bf16)
        carried[rows, :] = total_grad
        delta = twice[rows, :].astype(f32) * second_full[rows, :] + total_grad.astype(
            f32
        ) * diff_full[rows, :]
        stats[rows, 2:3] = jnp.sum(delta, axis=1, keepdims=True)
        return carry

    lax.fori_loop(0, QUARTERS, adjoint_step, 0, unroll=True)

    for copy in small_copies + big_copies + pass_copies:
        copy.wait_send()


def finish_kernel(
    n, grads, left_emb, right_emb, hidden, residual, diffused, second, twice, carried, stats, mix_big,
    layer_out_to, grad_src_to, grad_dst_to, grad_mix_to,
    layer_out, grad_src, grad_dst, grad_mix, store_sem,
):
    me = lax.axis_index("sensor")
    rows_q = PIECE * n
    total = QUARTERS * rows_q
    stores = [
        pltpu.make_async_copy(source, target, store_sem.at[at])
        for at, (source, target) in enumerate(
            [
                (layer_out, layer_out_to), (grad_mix, grad_mix_to),
                (grad_src, grad_src_to), (grad_dst, grad_dst_to),
            ]
        )
    ]

    def own(ref):
        return jnp.concatenate(
            [
                ref[pl.ds(pl.multiple_of(q * rows_q + me * PIECE, PIECE), PIECE), :]
                for q in range(QUARTERS)
            ],
            axis=0,
        )

    own_hidden, own_diff, own_second = own(hidden), own(diffused), own(second)
    own_left, own_right, own_stats = own(left_emb), own(right_emb), own(stats)
    own_residual = own(residual)
    for b in range(3):
        lanes = slice(128 * b, 128 * (b + 1))
        features = jnp.concatenate(
            [own_hidden[:, lanes], own_diff[:, lanes], own_second[:, lanes]], axis=1
        )
        layer_out[:, lanes] = (own_residual[:, lanes].astype(f32) + nn(features, mix_big[...])).astype(
            bf16
        )

    stores[0].start()

    mixed = jnp.zeros((128, 384), f32)
    for b in range(3):
        lanes = slice(128 * b, 128 * (b + 1))
        features = jnp.concatenate([hidden[:, lanes], diffused[:, lanes], second[:, lanes]], axis=1)
        mixed = mixed + tn(grads[:, :, lanes].reshape(total, 128), features)
    for k in range(3):
        grad_mix[:, 32 * k : 32 * (k + 1)] = sum(
            mixed[32 * t : 32 * (t + 1), 128 * k + 32 * t : 128 * k + 32 * (t + 1)]
            for t in range(4)
        )
    stores[1].start()

    def score_grad(scores, stat, products):
        shares = jnp.exp(jnp.maximum(scores, 0.0) - stat[:, 0:1]) * stat[:, 1:2]
        return halves(jnp.where(scores > 0.0, shares * (products - stat[:, 2:3]), 0.0))

    high, low = score_grad(
        nt(own_left, right_emb[...]),
        own_stats,
        nt(own(twice), diffused[...]) + nt(own(carried), hidden[...]),
    )
    summed = (nn(high, right_emb[...]) + nn(low, right_emb[...])).T
    grad_src[...] = summed[0:10, :] + summed[16:26, :] + summed[48:58, :]
    stores[2].start()

    high, low = score_grad(
        nt(left_emb[...], own_right),
        stats[...],
        nt(twice[...], own_diff) + nt(carried[...], own_hidden),
    )
    summed = tn(left_emb[...], high) + tn(left_emb[...], low)
    grad_dst[...] = summed[0:10, :] + summed[32:42, :] + summed[64:74, :]
    stores[3].start()
    for store in stores:
        store.wait()


def whole_in_kernel(
    series, starts, sensor_order, emb_src, emb_dst, start_proj, conv_weight, mix_weight, out_grad
):
    n = lax.axis_size("sensor")
    total = 48 * n
    vmem = pl.BlockSpec(memory_space=pltpu.VMEM)
    anywhere = pl.BlockSpec(memory_space=pltpu.HBM)
    dma = pltpu.SemaphoreType.DMA
    wide = jax.ShapeDtypeStruct((total, 384), bf16)
    lane = jax.ShapeDtypeStruct((total, 128), bf16)
    operands = (
        series.T, sensor_order.reshape(1, -1), emb_src, emb_dst, start_proj, conv_weight,
        mix_weight.T, out_grad,
    )
    operands = tuple(pltpu.with_memory_space_constraint(operand, pltpu.HBM) for operand in operands)
    held = pl.pallas_call(
        lambda *refs: gather_kernel(n, *refs),
        out_shape=(
            jax.ShapeDtypeStruct((QUARTERS, PIECE * n, 384), bf16),
            lane, lane, wide, wide, wide, wide, wide, wide,
            jax.ShapeDtypeStruct((total, 128), f32),
            jax.ShapeDtypeStruct((384, 128), bf16),
        ),
        in_specs=[pl.BlockSpec(memory_space=pltpu.SMEM)] + [anywhere] * 8,
        out_specs=(vmem,) * 11,
        scratch_shapes=[pltpu.VMEM(operand.shape, operand.dtype) for operand in operands]
        + [
            pltpu.VMEM((128, 128), f32),
            pltpu.VMEM((PIECE * n, 128), f32),
            pltpu.VMEM((total, 128), f32),
            pltpu.VMEM((total, 128), bf16),
            pltpu.VMEM((total, total), bf16),
            pltpu.VMEM((total, 384), f32),
            pltpu.VMEM((total, 384), f32),
            pltpu.VMEM((total, 384), bf16),
            dma((8,)),
            dma((n,)),
            dma((n,)),
            dma((n // 2,)),
            dma((n // 2,)),
            dma((n // 2,)),
            dma((n // 2,)),
        ],
        compiler_params=pltpu.CompilerParams(
            collective_id=0, has_side_effects=True, vmem_limit_bytes=32 * 2**20
        ),
    )(starts, *operands)
    outs = (
        jax.ShapeDtypeStruct((48, 384), bf16),
        jax.ShapeDtypeStruct((10, 48), f32),
        jax.ShapeDtypeStruct((10, 48), f32),
        jax.ShapeDtypeStruct((32, 96), f32),
    )
    layer_out, grad_src, grad_dst, grad_mix = pl.pallas_call(
        lambda *refs: finish_kernel(n, *refs),
        out_shape=outs,
        in_specs=[vmem] * 11,
        out_specs=(anywhere,) * 4,
        scratch_shapes=[pltpu.VMEM(out.shape, out.dtype) for out in outs] + [dma((4,))],
        compiler_params=pltpu.CompilerParams(vmem_limit_bytes=32 * 2**20),
    )(*held)
    return layer_out, grad_src, grad_dst, grad_mix.T


def layer_on_device(*operands):
    if lax.axis_size("sensor") == 16 and operands[2].shape[0] == 48:
        return whole_in_kernel(*operands)
    return per_device(*operands)


def solution(mesh):
    placed = (
        P(None, ("groups", "sensor")),
        P("groups"),
        P(("groups", "sensor")),
        P(None, ("groups", "sensor")),
        P(None, ("groups", "sensor")),
        P(),
        P(),
        P(),
        P(("groups", "sensor"), None),
    )
    return jax.shard_map(
        layer_on_device,
        mesh=mesh,
        in_specs=placed,
        out_specs=(
            P(("groups", "sensor"), None),
            P(None, ("groups", "sensor")),
            P(None, ("groups", "sensor")),
            P("groups", None),
        ),
        check_vma=False,
    )
```

```python
import math

import jax
import jax.numpy as jnp
from jax import lax
from jax.experimental import pallas as pl
from jax.experimental.pallas import tpu as pltpu
from jax.sharding import PartitionSpec as P

STEPS = 12


highest = lax.Precision.HIGHEST


def front(readings, start_proj, conv_weight):
    sensors_here = readings.shape[0]
    channels = start_proj.shape[1]
    padded = jnp.concatenate(
        [jnp.zeros(readings.shape[:-1] + (1,), jnp.float32), readings], axis=-1
    )
    inputs = (padded[..., None] * start_proj[0] + start_proj[1]).astype(jnp.bfloat16)
    paired = jnp.concatenate([inputs[:, :, :-1, :], inputs[:, :, 1:, :]], axis=-1).reshape(
        -1, 2 * channels
    )
    gate_terms = jnp.dot(paired, conv_weight, preferred_element_type=jnp.float32)
    hidden = (jnp.tanh(gate_terms[:, :channels]) * jax.nn.sigmoid(gate_terms[:, channels:])).astype(
        jnp.bfloat16
    )
    return (hidden.reshape(sensors_here, -1), inputs[:, :, 1:, :].reshape(sensors_here, -1))


def mixing(residual, hidden, diffused, second, mix_weight):
    channels = mix_weight.shape[1]
    stacked = jnp.concatenate(
        [member.reshape(-1, channels) for member in (hidden, diffused, second)], axis=1
    )
    summed = residual.reshape(-1, channels).astype(jnp.float32) + jnp.dot(
        stacked, mix_weight, preferred_element_type=jnp.float32
    )
    return (summed.astype(jnp.bfloat16).reshape(hidden.shape[0], -1), stacked)


def channel_grads(out_grad, mix_weight):
    channels = mix_weight.shape[1]
    row_count = out_grad.shape[0]
    flat_grad = out_grad.reshape(-1, channels)
    dims = (((1,), (1,)), ((), ()))
    grad_once = lax.dot_general(
        flat_grad, mix_weight[channels : 2 * channels], dims, preferred_element_type=jnp.float32
    )
    grad_twice = lax.dot_general(
        flat_grad, mix_weight[2 * channels :], dims, preferred_element_type=jnp.float32
    )
    return (
        grad_once.astype(jnp.bfloat16).reshape(row_count, -1),
        grad_twice.astype(jnp.bfloat16).reshape(row_count, -1),
    )


def tile_probs(rows_emb, cols_emb, row_max, row_total):
    scores = jnp.einsum("ei,ej->ij", rows_emb, cols_emb, precision=highest)
    shares = jnp.exp(jnp.maximum(scores, 0.0) - row_max[:, None]) / row_total[:, None]
    return (scores, shares)


def pair_dot(left, right):
    return lax.dot_general(
        left, right, (((1,), (1,)), ((), ())), preferred_element_type=jnp.float32
    )


def in_blocks(step_fn, status, members, axis_dim):
    amount = members[0].shape[axis_dim]
    span_size = math.gcd(amount, 512)

    def advance(position, current):
        opening = position * span_size
        sliced = tuple(
            (lax.dynamic_slice_in_dim(member, opening, span_size, axis_dim) for member in members)
        )
        return step_fn(current, sliced, opening)

    return lax.fori_loop(0, amount // span_size, advance, status)


def score_grads(status, emb_src, cols_dst, offset, scores, shares, dweights):
    grad_rows, grad_cols = status
    dscore = jnp.where(scores > 0.0, shares * dweights, 0.0)
    grad_rows = grad_rows + jnp.einsum("ej,ij->ei", cols_dst, dscore, precision=highest)
    span_size = dscore.shape[1]
    current = lax.dynamic_slice_in_dim(grad_cols, offset, span_size, 1)
    added = current + jnp.einsum("ei,ij->ej", emb_src, dscore, precision=highest)
    return (grad_rows, lax.dynamic_update_slice_in_dim(grad_cols, added, offset, 1))


def per_device(
    series, starts, sensor_order, emb_src, emb_dst, start_proj, conv_weight, mix_weight, out_grad
):
    local_rows = sensor_order.shape[0]
    embed_dim = emb_src.shape[0]
    channels = start_proj.shape[1]
    all_rows = local_rows * lax.axis_size("sensor")
    windows = jax.vmap(lambda first_step: lax.dynamic_slice_in_dim(series, first_step, STEPS, 0))(
        starts
    )
    flat_windows = windows.reshape(-1, local_rows)
    window_rows = flat_windows.shape[0]

    def pick_step(status, members, offset):
        readings_sum, dst_all = status
        block_windows, block_dst = members
        span_size = block_windows.shape[1]
        onehot = (sensor_order[:, None] == offset + lax.iota(jnp.int32, span_size)[None, :]).astype(
            jnp.float32
        )
        readings_sum = readings_sum + jnp.einsum(
            "wj,pj->wp", block_windows, onehot, precision=highest
        )
        return (readings_sum, lax.dynamic_update_slice_in_dim(dst_all, block_dst, offset, 1))

    readings_sum, dst_all = in_blocks(
        pick_step,
        (
            jnp.zeros((window_rows, local_rows), jnp.float32),
            jnp.zeros((embed_dim, all_rows), jnp.float32),
        ),
        (
            lax.all_gather(flat_windows, "sensor", axis=1, tiled=True),
            lax.all_gather(emb_dst, "sensor", axis=1, tiled=True),
        ),
        1,
    )
    readings = readings_sum.T.reshape(local_rows, -1, STEPS)
    hidden, residual = front(readings, start_proj, conv_weight)
    feat_cols = hidden.shape[1]
    span_all = math.gcd(all_rows, 512)

    def stat_step(position, current):
        best_score, summed = current
        cols_dst = lax.dynamic_slice_in_dim(dst_all, position * span_all, span_all, 1)
        scores = jnp.maximum(jnp.einsum("ei,ej->ij", emb_src, cols_dst, precision=highest), 0.0)
        new_best = jnp.maximum(best_score, jnp.max(scores, axis=1))
        summed = summed * jnp.exp(best_score - new_best) + jnp.sum(
            jnp.exp(scores - new_best[:, None]), axis=1
        )
        return (new_best, summed)

    row_max, row_total = lax.fori_loop(
        0,
        all_rows // span_all,
        stat_step,
        (jnp.zeros((local_rows,), jnp.float32), jnp.zeros((local_rows,), jnp.float32)),
    )
    grad_once, grad_twice = channel_grads(out_grad, mix_weight)

    def spread_step(status, members, offset):
        block_feat = members[0]
        cols_dst = lax.dynamic_slice_in_dim(dst_all, offset, block_feat.shape[0], 1)
        scores, shares = tile_probs(emb_src, cols_dst, row_max, row_total)
        return status + jnp.dot(
            shares.astype(jnp.bfloat16), block_feat, preferred_element_type=jnp.float32
        )

    first_init = jnp.zeros((local_rows, feat_cols), jnp.float32)
    first_result = in_blocks(
        spread_step, first_init, (lax.all_gather(hidden, "sensor", axis=0, tiled=True),), 0
    )
    diffused = first_result.astype(jnp.bfloat16)

    def plain_step(status, members, offset):
        accumulated, grad_rows, grad_cols = status
        return (spread_step(accumulated, members, offset), grad_rows, grad_cols)

    second_init = (
        jnp.zeros((local_rows, feat_cols), jnp.float32),
        jnp.zeros((embed_dim, local_rows), jnp.float32),
        jnp.zeros((embed_dim, all_rows), jnp.float32),
    )
    second_result = in_blocks(
        plain_step, second_init, (lax.all_gather(diffused, "sensor", axis=0, tiled=True),), 0
    )
    second_full, grad_rows, grad_cols = second_result
    second = second_full.astype(jnp.bfloat16)
    layer_out, stacked = mixing(residual, hidden, diffused, second, mix_weight)
    mix_part = lax.dot_general(
        stacked,
        out_grad.reshape(-1, channels),
        (((0,), (0,)), ((), ())),
        preferred_element_type=jnp.float32,
    )
    span_size = math.gcd(lax.axis_size("sensor") * local_rows, 512)

    def piece_term(position):
        cols_dst = lax.dynamic_slice_in_dim(dst_all, position * span_size, span_size, 1)
        scores, shares = tile_probs(emb_src, cols_dst, row_max, row_total)
        return lax.dot_general(
            shares.astype(jnp.bfloat16),
            grad_twice,
            (((0,), (0,)), ((), ())),
            preferred_element_type=jnp.float32,
        )

    adjoint_sum = lax.psum_scatter(
        lax.map(
            piece_term,
            jnp.arange(lax.axis_size("sensor") * local_rows // span_size, dtype=jnp.int32),
        ).reshape(lax.axis_size("sensor") * local_rows, -1),
        "sensor",
        scatter_dimension=0,
        tiled=True,
    )
    carried = (grad_once.astype(jnp.float32) + adjoint_sum).astype(jnp.bfloat16)
    row_delta = jnp.sum(
        grad_twice.astype(jnp.float32) * second_full + carried.astype(jnp.float32) * first_result,
        axis=1,
    )

    def pair_step(status, members, offset):
        block_hidden, block_diff = members
        cols_dst = lax.dynamic_slice_in_dim(dst_all, offset, block_hidden.shape[0], 1)
        scores, shares = tile_probs(emb_src, cols_dst, row_max, row_total)
        dweights = (
            pair_dot(grad_twice, block_diff) + pair_dot(carried, block_hidden) - row_delta[:, None]
        )
        return score_grads(status, emb_src, cols_dst, offset, scores, shares, dweights)

    grad_rows, grad_cols = in_blocks(
        pair_step,
        (grad_rows, grad_cols),
        (
            lax.all_gather(hidden, "sensor", axis=0, tiled=True),
            lax.all_gather(diffused, "sensor", axis=0, tiled=True),
        ),
        0,
    )
    grad_dst = lax.psum_scatter(grad_cols, "sensor", scatter_dimension=1, tiled=True)
    grad_mix = lax.psum(mix_part, "sensor")
    return (layer_out, grad_rows, grad_dst, grad_mix)


PIECE = 16
QUARTERS = 3
NT = (((1,), (1,)), ((), ()))
TN = (((0,), (0,)), ((), ()))
f32 = jnp.float32
bf16 = jnp.bfloat16


def iota(shape, dim):
    return lax.broadcasted_iota(jnp.int32, shape, dim)


def ones_where(mask):
    return jnp.where(mask, 1.0, 0.0).astype(bf16)


def nn(left, right):
    return jnp.dot(left, right, preferred_element_type=f32)


def nt(left, right):
    return lax.dot_general(left, right, NT, preferred_element_type=f32)


def tn(left, right):
    return lax.dot_general(left, right, TN, preferred_element_type=f32)


def halves(value):
    high = value.astype(bf16)
    return high, (value - high.astype(f32)).astype(bf16)


def thirds(value):
    high, middle = halves(value)
    return high, middle, (value - high.astype(f32) - middle.astype(f32)).astype(bf16)


def selection(q):
    col = iota((1, 384), 1)
    tile, lane = col >> 7, col & 127
    u, e = lane >> 4, lane & 15
    left = jnp.where((u == 2) | (u == 5), 1, jnp.where(u == 4, 2, 0)) * 128 + e
    right = jnp.where((u == 1) | (u == 5), 1, jnp.where(u == 3, 2, 0)) * 128 + e + 10
    window = u * 128 + e + 20
    wanted = jnp.where(tile == 0, left, jnp.where(tile == 1, right, window))
    blocks, width = jnp.where(tile == 2, 3, 6), jnp.where(tile == 2, 12, 10)
    wanted = jnp.where((u < blocks) & (e < width), wanted + 40 * q, -1)
    number = jnp.where(col == 320, 32 + 40 * q, -1)
    row = iota((384, 384), 0)
    return ones_where((row == wanted) | ((row & 127) == number))


def gather_kernel(
    n, starts, series_in, order_in, src_in, dst_in, proj_in, conv_in, mix_in, out_grad_in,
    grads, left_emb, right_emb, hidden, residual, diffused, second, twice, carried, stats, mix_out,
    series, order, src, dst, start_proj, conv, mix, out_grad,
    packed, small, window_f, window_b, adj, diff_full, second_full, once,
    load_sem, small_send, small_recv, big_send, big_recv, pass_send, pass_recv,
):
    loads = [
        pltpu.make_async_copy(source, target, load_sem.at[at])
        for at, (source, target) in enumerate(
            [
                (series_in, series), (order_in, order), (src_in, src), (dst_in, dst),
                (out_grad_in, out_grad), (conv_in, conv), (mix_in, mix), (proj_in, start_proj),
            ]
        )
    ]
    for load in loads[:4]:
        load.start()
    me = lax.axis_index("sensor")
    rows_q = PIECE * n
    total = QUARTERS * rows_q
    barrier = pltpu.get_barrier_semaphore()
    for k in range(1, n):
        pl.semaphore_signal(
            barrier, inc=1, device_id={"sensor": lax.rem(me + k, n)},
            device_id_type=pl.DeviceIdType.MESH,
        )
    for load in loads[4:]:
        load.start()
    mine = pl.multiple_of(me * PIECE, PIECE)

    wanted = ones_where(iota((16, series.shape[1]), 1) == iota((16, series.shape[1]), 0) + starts[0])
    for load in loads[:4]:
        load.wait()
    window = sum(nt(wanted, part) for part in thirds(series[...]))[0:STEPS, :]
    block = jnp.concatenate(
        [src[...], dst[...], window, order[...].astype(f32), jnp.zeros((7, 48), f32)], axis=0
    )
    packed[...] = jnp.zeros_like(packed)
    for q in range(QUARTERS):
        packed[40 * q : 40 * q + 40, 0:PIECE] = block[:, PIECE * q : PIECE * (q + 1)]
    small[pl.ds(mine, PIECE), :] = packed[...].T[0:PIECE, :]
    loads[4].wait()
    for q in range(QUARTERS):
        grads[q, pl.ds(mine, PIECE), :] = out_grad[PIECE * q : PIECE * (q + 1), :]

    pl.semaphore_wait(barrier, n - 1)

    def remote(where, send, recv, peer):
        return pltpu.make_async_remote_copy(
            src_ref=where, dst_ref=where, send_sem=send, recv_sem=recv,
            device_id={"sensor": peer}, device_id_type=pl.DeviceIdType.MESH,
        )

    small_copies = []
    sibling = me + 1 - 2 * lax.rem(me, 2)
    for k in range(n // 2):
        copy = remote(
            small.at[pl.ds(mine, PIECE), :], small_send.at[k], small_recv.at[k],
            sibling if k == 0 else lax.rem(me + 2 * k, n),
        )
        copy.start()
        small_copies.append(copy)
    big_copies = []
    for k in range(n // 2):
        copy = remote(
            grads.at[:, pl.ds(mine, PIECE), :], big_send.at[k], big_recv.at[k],
            sibling if k == 0 else lax.rem(me + 2 * k, n),
        )
        copy.start()
        big_copies.append(copy)

    for load in loads[5:]:
        load.wait()

    spread = ones_where(iota((256, 64), 1) == (iota((256, 64), 0) >> 7) * 32 + (iota((256, 64), 0) & 31))
    gather = ones_where(iota((64, 256), 0) == (iota((64, 256), 1) >> 7) * 32 + (iota((64, 256), 1) & 31))
    conv_big = nn(nn(spread, conv[...]).astype(bf16), gather)
    conv_big = jnp.where(
        ((iota((256, 256), 0) & 127) >> 5) == ((iota((256, 256), 1) & 127) >> 5), conv_big, 0.0
    ).astype(bf16)
    spread = ones_where(iota((384, 96), 1) == (iota((384, 96), 0) >> 7) * 32 + (iota((384, 96), 0) & 31))
    gather = ones_where(iota((32, 128), 0) == (iota((32, 128), 1) & 31))
    mix_big = nn(nt(spread, mix[...]).astype(bf16), gather)
    mix_big = jnp.where(
        ((iota((384, 128), 0) & 127) >> 5) == (iota((384, 128), 1) >> 5), mix_big, 0.0
    ).astype(bf16)
    mix_out[...] = mix_big
    proj = jnp.concatenate([start_proj[...]] * 4, axis=1)
    weight, bias = proj[0:1, :], proj[1:2, :]
    at = iota((128, 768), 0)
    col = iota((128, 768), 1)
    step = jnp.where(col < 384, (col >> 5) - 1, (col - 384) >> 5)
    expand = ones_where(((at & 15) == step) & (at < 48))
    numbers = jnp.concatenate(
        [
            48 * (iota((1, rows_q), 1) >> 4) + PIECE * q + (iota((1, rows_q), 1) & 15)
            for q in range(QUARTERS)
        ],
        axis=1,
    ).astype(f32)

    chosen = [selection(q) for q in range(QUARTERS)]
    for k in range(1, n // 2):
        small_copies[k].wait_recv()
        origin = pl.multiple_of(lax.rem(me + n - 2 * k, n) * PIECE, PIECE)
        copy = remote(
            small.at[pl.ds(origin, PIECE), :],
            small_send.at[n // 2 + k],
            small_recv.at[n // 2 + k],
            sibling,
        )
        copy.start()
        small_copies.append(copy)
    small_copies[0].wait_recv()
    for copy in small_copies[n // 2 :]:
        copy.wait_recv()

    parts = jnp.concatenate(thirds(small[...]), axis=1)
    for q in range(QUARTERS):
        taken = nn(parts, chosen[q])
        rows = slice(q * rows_q, (q + 1) * rows_q)
        left_emb[rows, :] = taken[:, 0:128].astype(bf16)
        right_emb[rows, :] = taken[:, 128:256].astype(bf16)
        window_f[rows, :] = taken[:, 256:384]
        window_b[rows, :] = taken[:, 256:384].astype(bf16)

    def chunk(q):
        return pl.ds(pl.multiple_of(q * rows_q, rows_q), rows_q)

    def front_step(q, carry):
        rows = chunk(q)
        onehot = ones_where(window_f[rows, 64:65] == numbers)
        picked = nn(onehot, window_b[...]).astype(bf16)
        wide = nn(picked, expand)
        for b in range(3):
            lanes = slice(128 * b, 128 * (b + 1))
            before = (wide[:, 128 * b : 128 * (b + 1)] * weight + bias).astype(bf16)
            after = (wide[:, 384 + 128 * b : 512 + 128 * b] * weight + bias).astype(bf16)
            residual[rows, lanes] = after
            terms = nn(jnp.concatenate([before, after], axis=1), conv_big)
            gated = jnp.tanh(terms[:, :128]) * (0.5 * jnp.tanh(0.5 * terms[:, 128:]) + 0.5)
            hidden[rows, lanes] = gated.astype(bf16)
        return carry

    lax.fori_loop(0, QUARTERS, front_step, 0, unroll=True)

    def first_step(q, carry):
        rows = chunk(q)
        positive = jnp.maximum(nt(left_emb[rows, :], right_emb[...]), 0.0)
        top = jnp.max(positive, axis=1, keepdims=True)
        terms = jnp.exp(positive - top)
        inverse = 1.0 / jnp.sum(terms, axis=1, keepdims=True)
        weights = (terms * inverse).astype(bf16)
        adj[rows, :] = weights
        stats[rows, 0:1] = top
        stats[rows, 1:2] = inverse
        result = nn(weights, hidden[...])
        diff_full[rows, :] = result
        diffused[rows, :] = result.astype(bf16)
        return carry

    lax.fori_loop(0, QUARTERS, first_step, 0, unroll=True)

    pass_copies = []
    for k in range(1, n // 2):
        big_copies[k].wait_recv()
        origin = pl.multiple_of(lax.rem(me + n - 2 * k, n) * PIECE, PIECE)
        copy = remote(
            grads.at[:, pl.ds(origin, PIECE), :], pass_send.at[k], pass_recv.at[k], sibling
        )
        copy.start()
        pass_copies.append(copy)

    def second_step(q, carry):
        rows = chunk(q)
        result = nn(adj[rows, :], diffused[...])
        second_full[rows, :] = result
        second[rows, :] = result.astype(bf16)
        return carry

    lax.fori_loop(0, QUARTERS, second_step, 0, unroll=True)

    big_copies[0].wait_recv()
    for copy in pass_copies:
        copy.wait_recv()

    def channel_step(q, carry):
        rows = chunk(q)
        given = grads[q]
        for b in range(3):
            lanes = slice(128 * b, 128 * (b + 1))
            both = nt(given[:, lanes], mix_big[128:384, :]).astype(bf16)
            once[rows, lanes] = both[:, :128]
            twice[rows, lanes] = both[:, 128:]
        return carry

    lax.fori_loop(0, QUARTERS, channel_step, 0, unroll=True)

    def adjoint_step(q, carry):
        rows = chunk(q)
        back = tn(adj[:, rows], twice[...])
        total_grad = (once[rows, :].astype(f32) + back).astype(bf16)
        carried[rows, :] = total_grad
        delta = twice[rows, :].astype(f32) * second_full[rows, :] + total_grad.astype(
            f32
        ) * diff_full[rows, :]
        stats[rows, 2:3] = jnp.sum(delta, axis=1, keepdims=True)
        return carry

    lax.fori_loop(0, QUARTERS, adjoint_step, 0, unroll=True)

    for copy in small_copies + big_copies + pass_copies:
        copy.wait_send()


def finish_kernel(
    n, grads, left_emb, right_emb, hidden, residual, diffused, second, twice, carried, stats, mix_big,
    layer_out_to, grad_src_to, grad_dst_to, grad_mix_to,
    layer_out, grad_src, grad_dst, grad_mix, store_sem,
):
    me = lax.axis_index("sensor")
    rows_q = PIECE * n
    total = QUARTERS * rows_q
    stores = [
        pltpu.make_async_copy(source, target, store_sem.at[at])
        for at, (source, target) in enumerate(
            [
                (layer_out, layer_out_to), (grad_mix, grad_mix_to),
                (grad_src, grad_src_to), (grad_dst, grad_dst_to),
            ]
        )
    ]

    def own(ref):
        return jnp.concatenate(
            [
                ref[pl.ds(pl.multiple_of(q * rows_q + me * PIECE, PIECE), PIECE), :]
                for q in range(QUARTERS)
            ],
            axis=0,
        )

    own_hidden, own_diff, own_second = own(hidden), own(diffused), own(second)
    own_left, own_right, own_stats = own(left_emb), own(right_emb), own(stats)
    own_residual = own(residual)
    for b in range(3):
        lanes = slice(128 * b, 128 * (b + 1))
        features = jnp.concatenate(
            [own_hidden[:, lanes], own_diff[:, lanes], own_second[:, lanes]], axis=1
        )
        layer_out[:, lanes] = (own_residual[:, lanes].astype(f32) + nn(features, mix_big[...])).astype(
            bf16
        )

    stores[0].start()

    mixed = jnp.zeros((128, 384), f32)
    for b in range(3):
        lanes = slice(128 * b, 128 * (b + 1))
        features = jnp.concatenate([hidden[:, lanes], diffused[:, lanes], second[:, lanes]], axis=1)
        mixed = mixed + tn(grads[:, :, lanes].reshape(total, 128), features)
    for k in range(3):
        grad_mix[:, 32 * k : 32 * (k + 1)] = sum(
            mixed[32 * t : 32 * (t + 1), 128 * k + 32 * t : 128 * k + 32 * (t + 1)]
            for t in range(4)
        )
    stores[1].start()

    def score_grad(scores, stat, products):
        shares = jnp.exp(jnp.maximum(scores, 0.0) - stat[:, 0:1]) * stat[:, 1:2]
        return halves(jnp.where(scores > 0.0, shares * (products - stat[:, 2:3]), 0.0))

    high, low = score_grad(
        nt(own_left, right_emb[...]),
        own_stats,
        nt(own(twice), diffused[...]) + nt(own(carried), hidden[...]),
    )
    summed = (nn(high, right_emb[...]) + nn(low, right_emb[...])).T
    grad_src[...] = summed[0:10, :] + summed[16:26, :] + summed[48:58, :]
    stores[2].start()

    high, low = score_grad(
        nt(left_emb[...], own_right),
        stats[...],
        nt(twice[...], own_diff) + nt(carried[...], own_hidden),
    )
    summed = tn(left_emb[...], high) + tn(left_emb[...], low)
    grad_dst[...] = summed[0:10, :] + summed[32:42, :] + summed[64:74, :]
    stores[3].start()
    for store in stores:
        store.wait()


def whole_in_kernel(
    series, starts, sensor_order, emb_src, emb_dst, start_proj, conv_weight, mix_weight, out_grad
):
    n = lax.axis_size("sensor")
    total = 48 * n
    vmem = pl.BlockSpec(memory_space=pltpu.VMEM)
    anywhere = pl.BlockSpec(memory_space=pltpu.HBM)
    dma = pltpu.SemaphoreType.DMA
    wide = jax.ShapeDtypeStruct((total, 384), bf16)
    lane = jax.ShapeDtypeStruct((total, 128), bf16)
    operands = (
        series.T, sensor_order.reshape(1, -1), emb_src, emb_dst, start_proj, conv_weight,
        mix_weight.T, out_grad,
    )
    operands = tuple(pltpu.with_memory_space_constraint(operand, pltpu.HBM) for operand in operands)
    held = pl.pallas_call(
        lambda *refs: gather_kernel(n, *refs),
        out_shape=(
            jax.ShapeDtypeStruct((QUARTERS, PIECE * n, 384), bf16),
            lane, lane, wide, wide, wide, wide, wide, wide,
            jax.ShapeDtypeStruct((total, 128), f32),
            jax.ShapeDtypeStruct((384, 128), bf16),
        ),
        in_specs=[pl.BlockSpec(memory_space=pltpu.SMEM)] + [anywhere] * 8,
        out_specs=(vmem,) * 11,
        scratch_shapes=[pltpu.VMEM(operand.shape, operand.dtype) for operand in operands]
        + [
            pltpu.VMEM((128, 128), f32),
            pltpu.VMEM((PIECE * n, 128), f32),
            pltpu.VMEM((total, 128), f32),
            pltpu.VMEM((total, 128), bf16),
            pltpu.VMEM((total, total), bf16),
            pltpu.VMEM((total, 384), f32),
            pltpu.VMEM((total, 384), f32),
            pltpu.VMEM((total, 384), bf16),
            dma((8,)),
            dma((n,)),
            dma((n,)),
            dma((n // 2,)),
            dma((n // 2,)),
            dma((n // 2,)),
            dma((n // 2,)),
        ],
        compiler_params=pltpu.CompilerParams(
            collective_id=0, has_side_effects=True, vmem_limit_bytes=32 * 2**20
        ),
    )(starts, *operands)
    outs = (
        jax.ShapeDtypeStruct((48, 384), bf16),
        jax.ShapeDtypeStruct((10, 48), f32),
        jax.ShapeDtypeStruct((10, 48), f32),
        jax.ShapeDtypeStruct((32, 96), f32),
    )
    layer_out, grad_src, grad_dst, grad_mix = pl.pallas_call(
        lambda *refs: finish_kernel(n, *refs),
        out_shape=outs,
        in_specs=[vmem] * 11,
        out_specs=(anywhere,) * 4,
        scratch_shapes=[pltpu.VMEM(out.shape, out.dtype) for out in outs] + [dma((4,))],
        compiler_params=pltpu.CompilerParams(vmem_limit_bytes=32 * 2**20),
    )(*held)
    return layer_out, grad_src, grad_dst, grad_mix.T


def layer_on_device(*operands):
    if lax.axis_size("sensor") == 16 and operands[2].shape[0] == 48:
        return whole_in_kernel(*operands)
    return per_device(*operands)


def solution(mesh):
    placed = (
        P(None, ("groups", "sensor")),
        P("groups"),
        P(("groups", "sensor")),
        P(None, ("groups", "sensor")),
        P(None, ("groups", "sensor")),
        P(),
        P(),
        P(),
        P(("groups", "sensor"), None),
    )
    return jax.shard_map(
        layer_on_device,
        mesh=mesh,
        in_specs=placed,
        out_specs=(
            P(("groups", "sensor"), None),
            P(None, ("groups", "sensor")),
            P(None, ("groups", "sensor")),
            P("groups", None),
        ),
        check_vma=False,
    )
```
